512 devices in a mesh: dp: 32 (over z, y_hi), tensor: 16 (over x, y_lo, core).
Axes of the slice: x: 4, y: 4 (y_hi: 2, y_lo: 2; y = y_hi * 2 + y_lo), z: 16, core: 2. Of those that a mesh axis runs over, the one named last changes fastest.
Arguments:
- residual: bfloat16 [4096, 2048], P(('dp', 'tensor')), may hold values from -6 to 6
- norm_gain: float32 [2048], replicated, may hold values from 0.1 to 1.9
- gate_weight: bfloat16 [2048, 7168], P(None, 'tensor'), may hold values from -0.125 to 0.125
- up_weight: bfloat16 [2048, 7168], P(None, 'tensor'), may hold values from -0.125 to 0.125
- hidden_grad: bfloat16 [4096, 7168], P('dp', 'tensor'), may hold values from -6 to 6
Outputs:
- residual_grad: bfloat16 [4096, 2048], P(('dp', 'tensor'))
- gate_weight_grad: bfloat16 [2048, 7168], P('dp', 'tensor')
- up_weight_grad: bfloat16 [2048, 7168], P('dp', 'tensor')
The draws below stay inside these ranges and needn't reach their ends.
All inputs are finite; a program needn't handle non-finite values.
Results may differ from the reference program's by a relative error of at most 0.024.
Values may be sent and summed in bfloat16 or wider, within the bound.
No kernel may reach another device: no remote copies, remote signals or barrier semaphores. Data moves between devices by JAX's collectives and lax.ppermute only.
A program may use at most 64 MiB of HBM per device.

```python
import math
import jax
import jax.numpy as jnp
from jax import lax

D = 2048
FF = 7168
ROWS = 128
TOKENS = 4096
N_DP = 32
N_TENSOR = 16


def block_levels(rng, extent, split, smallest, high):
    level, own = 1.0, jax.random.fold_in(rng, 6)
    for axis_at, shards_of in split:
        heights = jnp.exp(jax.random.uniform(jax.random.fold_in(own, axis_at), (shards_of,), jnp.float32, smallest / len(split), high / len(split)))
        level = level * jnp.repeat(heights, extent[axis_at] // shards_of).reshape([-1 if axis == axis_at else 1 for axis in range(len(extent))])
    return level


def gaussian(own_key, dims, scale, most, split=(), held_as=jnp.bfloat16):
    factor_of = block_levels(own_key, dims, split, -0.22, 0.18) if split else 1.0
    entries = jax.random.normal(own_key, dims, jnp.float32) * scale * factor_of
    return jnp.minimum(jnp.maximum(entries, -most), most).astype(held_as)


def setup_inputs(seed: int = 0) -> dict:
    key_of = jax.random.split(jax.random.key(seed), 6)
    residual = gaussian(key_of[0], (TOKENS, D), 1.0, 6.0, ((0, 512),))
    norm_gain = jnp.clip(1.0 + 0.18 * jax.random.normal(key_of[1], (D,), jnp.float32), 0.1, 1.9)
    gate_weight = gaussian(key_of[2], (D, FF), D ** -0.5, 0.125, ((1, 16),))
    up_weight = gaussian(key_of[3], (D, FF), D ** -0.5, 0.125, ((1, 16),))
    hidden_grad = gaussian(key_of[4], (TOKENS, FF), 1.0, 6.0, ((0, 32), (1, 16)))
    return {"residual": residual, "norm_gain": norm_gain, "gate_weight": gate_weight, "up_weight": up_weight, "hidden_grad": hidden_grad}


EPSILON = 1e-05

def normalize(residual):
    values = residual.astype(jnp.float32)
    inverse = lax.rsqrt(lax.optimization_barrier(jnp.mean(values * values, axis=-1, keepdims=True)) + EPSILON)
    return (values * inverse, inverse)

def reference(residual, norm_gain, gate_weight, up_weight, hidden_grad):
    scaled, inverse = normalize(residual)
    normed = (scaled * norm_gain).astype(jnp.bfloat16)
    factor = 1.0 / math.sqrt(TOKENS)
    block = FF // N_TENSOR
    gate_blocks = gate_weight.astype(jnp.float32).reshape(D, N_TENSOR, block)
    up_blocks = up_weight.astype(jnp.float32).reshape(D, N_TENSOR, block)
    normed_groups = normed.reshape(N_DP, ROWS, D)
    upstream_groups = hidden_grad.reshape(N_DP, ROWS, FF)

    def group_step(carry, pieces):
        gate_total, up_total = carry
        normed_rows, upstream_rows = pieces
        gate_value = jnp.dot(normed_rows, gate_weight, preferred_element_type=jnp.float32)
        up_value = jnp.dot(normed_rows, up_weight, preferred_element_type=jnp.float32)
        sigmoid_gate = jax.nn.sigmoid(gate_value)
        upstream = upstream_rows.astype(jnp.float32)
        up_grad = (upstream * gate_value * sigmoid_gate).astype(jnp.bfloat16)
        gate_grad = (upstream * up_value * sigmoid_gate * (1.0 + gate_value * (1.0 - sigmoid_gate))).astype(jnp.bfloat16)
        partial_value = jnp.einsum('rkf,dkf->krd', gate_grad.astype(jnp.float32).reshape(ROWS, N_TENSOR, block), gate_blocks)
        partial_value = partial_value + jnp.einsum('rkf,dkf->krd', up_grad.astype(jnp.float32).reshape(ROWS, N_TENSOR, block), up_blocks)
        normed_grad = lax.optimization_barrier(jnp.sum(lax.optimization_barrier(partial_value.astype(jnp.bfloat16)).astype(jnp.float32), axis=0))
        gate_part = jnp.dot(normed_rows.T, gate_grad, preferred_element_type=jnp.float32) * factor
        up_part = jnp.dot(normed_rows.T, up_grad, preferred_element_type=jnp.float32) * factor
        gate_total = gate_total + lax.optimization_barrier(gate_part.astype(jnp.bfloat16)).astype(jnp.float32)
        up_total = up_total + lax.optimization_barrier(up_part.astype(jnp.bfloat16)).astype(jnp.float32)
        return ((gate_total, up_total), normed_grad)
    zeros = jnp.zeros((D, FF), jnp.float32)
    (gate_total, up_total), normed_grad = lax.scan(group_step, (zeros, zeros), (normed_groups, upstream_groups))
    normed_grad = normed_grad.reshape(TOKENS, D)
    weighted = normed_grad * norm_gain
    residual_grad = ((weighted - scaled * lax.optimization_barrier(jnp.mean(weighted * scaled, axis=-1, keepdims=True))) * inverse).astype(jnp.bfloat16)
    return (residual_grad, gate_total.astype(jnp.bfloat16), up_total.astype(jnp.bfloat16))
```

```python
import jax
import jax.numpy as jnp
from jax import lax
from jax.sharding import Mesh
from jax.sharding import PartitionSpec as P

EPSILON = 1e-05
DP = ("z", "yh")
TENSOR = ("x", "yl", "core")


def normalize(residual):
    values = residual.astype(jnp.float32)
    inverse = lax.rsqrt(jnp.mean(values * values, axis=-1, keepdims=True) + EPSILON)
    return (values * inverse, inverse)


def contract_last(left, right):
    return lax.dot_general(
        left, right, (((1,), (1,)), ((), ())), preferred_element_type=jnp.float32
    )


def contract_first(left, right):
    return lax.dot_general(
        left, right, (((0,), (0,)), ((), ())), preferred_element_type=jnp.float32
    )


def gather_rows(block, axes, count):
    copies = jnp.broadcast_to(block[None], (count,) + block.shape)
    return lax.all_to_all(copies, axes, 0, 0, tiled=True).reshape(
        (count * block.shape[0],) + block.shape[1:]
    )


def scatter_sum(partial, axes, count):
    blocks = partial.reshape((count, partial.shape[0] // count) + partial.shape[1:])
    moved = lax.all_to_all(blocks, axes, 0, 0, tiled=True)
    return jnp.sum(moved.astype(jnp.float32), axis=0)


def shards(residual, norm_gain, gate_weight, up_weight, hidden_grad):
    n_tensor = lax.axis_size(TENSOR)
    scaled, inverse = normalize(residual)
    gathered = gather_rows(residual, TENSOR, n_tensor)
    normed = (normalize(gathered)[0] * norm_gain).astype(jnp.bfloat16)
    gate_value = jnp.dot(normed, gate_weight, preferred_element_type=jnp.float32)
    up_value = jnp.dot(normed, up_weight, preferred_element_type=jnp.float32)
    sigmoid_gate = jax.nn.sigmoid(gate_value)
    upstream = hidden_grad.astype(jnp.float32)
    up_grad = (upstream * gate_value * sigmoid_gate).astype(jnp.bfloat16)
    gate_grad = (
        upstream * up_value * sigmoid_gate * (1.0 + gate_value * (1.0 - sigmoid_gate))
    ).astype(jnp.bfloat16)
    factor = float(normed.shape[0] * lax.axis_size(DP)) ** (-0.5)
    both = jnp.concatenate([gate_grad, up_grad], axis=1)
    part = (contract_first(normed, both) * factor).astype(jnp.bfloat16)
    over_z = lax.psum_scatter(part, "z", scatter_dimension=0, tiled=True)
    total = scatter_sum(over_z, "yh", lax.axis_size("yh")).astype(jnp.bfloat16)
    width = gate_grad.shape[1]
    normed_grad = scatter_sum(
        (contract_last(gate_grad, gate_weight) + contract_last(up_grad, up_weight)).astype(
            jnp.bfloat16
        ),
        TENSOR,
        n_tensor,
    )
    weighted = normed_grad * norm_gain
    residual_grad = (
        (weighted - scaled * jnp.mean(weighted * scaled, axis=-1, keepdims=True)) * inverse
    ).astype(jnp.bfloat16)
    return (residual_grad, total[:, :width], total[:, width:])


def solution(mesh):
    fine = Mesh(mesh.devices.reshape(16, 2, 4, 2, 2), DP + TENSOR)
    return jax.shard_map(
        shards,
        mesh=fine,
        in_specs=(
            P(DP + TENSOR, None),
            P(),
            P(None, TENSOR),
            P(None, TENSOR),
            P(DP, TENSOR),
        ),
        out_specs=(P(DP + TENSOR, None), P(DP, TENSOR), P(DP, TENSOR)),
        check_vma=False,
    )
```

```python
import functools

import jax
import jax.numpy as jnp
from jax import lax
from jax.experimental import pallas as pl
from jax.experimental.pallas import tpu as pltpu
from jax.sharding import Mesh
from jax.sharding import PartitionSpec as P

EPSILON = 1e-05
DP = ("z", "yh")
TENSOR = ("x", "yl", "core")
HUBS = (-6, -3, 0, 3, 6)


def normalize(residual):
    values = residual.astype(jnp.float32)
    inverse = lax.rsqrt(jnp.mean(values * values, axis=-1, keepdims=True) + EPSILON)
    return (values * inverse, inverse)


def contract_last(left, right):
    return lax.dot_general(
        left, right, (((1,), (1,)), ((), ())), preferred_element_type=jnp.float32
    )


def contract_first(left, right):
    return lax.dot_general(
        left, right, (((0,), (0,)), ((), ())), preferred_element_type=jnp.float32
    )


def local_kernel(
    factor,
    nz,
    rows_ref,
    gain_ref,
    gate_ref,
    up_ref,
    own_ref,
    other_ref,
    ahead_ref,
    behind_ref,
    far_ref,
    hub_ref,
    gate_own_ref,
    up_own_ref,
    normed_ref,
    grads_ref,
):
    z = lax.axis_index("z")
    half = lax.axis_index("yh")
    rows = own_ref.shape[1]
    width = own_ref.shape[0]
    scaled = normalize(rows_ref[...])[0]
    normed_ref[...] = (scaled * gain_ref[...]).astype(jnp.bfloat16)
    normed = normed_ref[...]
    gate_value = contract_last(normed, gate_ref[...])
    up_value = contract_last(normed, up_ref[...])
    own = own_ref[...].astype(jnp.float32).T
    other = other_ref[...].astype(jnp.float32).T
    first = half == 0
    upstream = jnp.concatenate(
        [jnp.where(first, own, other), jnp.where(first, other, own)], axis=0
    )
    sigmoid_gate = jax.nn.sigmoid(gate_value)
    weighted = upstream * sigmoid_gate
    grads_ref[:, width:] = (weighted * gate_value).astype(jnp.bfloat16)
    grads_ref[:, :width] = (
        weighted * up_value * (1.0 + gate_value * (1.0 - sigmoid_gate))
    ).astype(jnp.bfloat16)
    start = pl.multiple_of(half * rows, rows)
    gate_own_ref[...] = grads_ref[pl.ds(start, rows), :width]
    up_own_ref[...] = grads_ref[pl.ds(start, rows), width:]
    grads = grads_ref[...]
    depth = far_ref.shape[0]

    def block(relative):
        chunk = lax.rem(z - relative + 2 * nz, nz)
        lanes = pl.ds(pl.multiple_of(chunk * 2 * depth, 2 * depth), 2 * depth)
        both = contract_first(normed_ref[:, lanes], grads) * factor
        return jnp.where(first, both[:depth], both[depth:]).astype(jnp.bfloat16)

    for at, hub in enumerate(HUBS):
        ahead_ref[at] = block(hub - 1)
        behind_ref[at] = block(hub + 1)
    far_ref[...] = block(nz // 2)
    for at, hub in enumerate(HUBS):
        hub_ref[at] = block(hub)


def shift(value, hops, nz):
    return lax.ppermute(value, "z", [(i, (i + hops) % nz) for i in range(nz)])


def shards(residual, norm_gain, gate_weight, up_weight, hidden_grad):
    nz, nh, nt = lax.axis_size("z"), lax.axis_size("yh"), lax.axis_size(TENSOR)
    rows, width = hidden_grad.shape
    features = residual.shape[1]
    depth = features // (nz * nh)
    f32, bf16 = jnp.float32, jnp.bfloat16
    own = hidden_grad.T
    other = lax.ppermute(own, "yh", [(0, 1), (1, 0)])
    copies = jnp.broadcast_to(residual[None], (nh * nt,) + residual.shape)
    gathered = lax.all_to_all(copies, ("yh",) + TENSOR, 0, 0, tiled=True)
    gathered = gathered.reshape(nh * rows, features)
    factor = float(rows * nz * nh) ** (-0.5)
    shape = jax.ShapeDtypeStruct
    hubs = len(HUBS)
    ahead, behind, far, hub, gate_own, up_own = pl.pallas_call(
        functools.partial(local_kernel, factor, nz),
        out_shape=(
            shape((hubs, depth, 2 * width), bf16),
            shape((hubs, depth, 2 * width), bf16),
            shape((depth, 2 * width), bf16),
            shape((hubs, depth, 2 * width), bf16),
            shape((rows, width), bf16),
            shape((rows, width), bf16),
        ),
        scratch_shapes=[
            pltpu.VMEM((nh * rows, features), bf16),
            pltpu.VMEM((nh * rows, 2 * width), bf16),
        ],
        compiler_params=pltpu.CompilerParams(vmem_limit_bytes=40 * 1024 * 1024),
        cost_estimate=pl.CostEstimate(
            flops=8 * nh * rows * features * width,
            bytes_accessed=8 * features * width,
            transcendentals=nh * rows * width,
        ),
        name="local",
    )(gathered, norm_gain.reshape(1, features), gate_weight.T, up_weight.T, own, other)

    from_behind = shift(ahead, 1, nz)
    from_ahead = shift(behind, -1, nz)
    from_far = shift(far, -2, nz)

    part = (contract_last(gate_own, gate_weight) + contract_last(up_own, up_weight)).astype(bf16)
    blocks = part.reshape(nt, rows // nt, features)
    moved = lax.all_to_all(blocks, TENSOR, 0, 0, tiled=True)

    sums = hub.astype(f32) + from_behind.astype(f32) + from_ahead.astype(f32)
    last = (sums[hubs - 1] + from_far.astype(f32)).astype(bf16)
    total = sums[2]
    total = total + shift(sums[0].astype(bf16), 6, nz).astype(f32)
    total = total + shift(sums[1].astype(bf16), 3, nz).astype(f32)
    total = total + shift(sums[3].astype(bf16), -3, nz).astype(f32)
    total = total + shift(last, -6, nz).astype(f32)
    total = total.astype(bf16)

    scaled, inverse = normalize(residual)
    normed_grad = jnp.sum(moved.astype(f32), axis=0)
    weighted = normed_grad * norm_gain
    residual_grad = (
        (weighted - scaled * jnp.mean(weighted * scaled, axis=-1, keepdims=True)) * inverse
    ).astype(bf16)
    return (residual_grad, total[:, :width], total[:, width:])


def solution(mesh):
    fine = Mesh(mesh.devices.reshape(16, 2, 4, 2, 2), DP + TENSOR)
    return jax.shard_map(
        shards,
        mesh=fine,
        in_specs=(
            P(DP + TENSOR, None),
            P(),
            P(None, TENSOR),
            P(None, TENSOR),
            P(DP, TENSOR),
        ),
        out_specs=(P(DP + TENSOR, None), P(DP, TENSOR), P(DP, TENSOR)),
        check_vma=False,
    )
```

```python
import functools

import jax
import jax.numpy as jnp
from jax import lax
from jax.experimental import pallas as pl
from jax.experimental.pallas import tpu as pltpu
from jax.sharding import Mesh
from jax.sharding import PartitionSpec as P

EPSILON = 1e-05
DP = ("z", "yh")
TENSOR = ("x", "yl", "core")
HUBS = (-6, -3, 0, 3, 6)


def normalize(residual):
    values = residual.astype(jnp.float32)
    inverse = lax.rsqrt(jnp.mean(values * values, axis=-1, keepdims=True) + EPSILON)
    return (values * inverse, inverse)


def contract_last(left, right):
    return lax.dot_general(
        left, right, (((1,), (1,)), ((), ())), preferred_element_type=jnp.float32
    )


def contract_first(left, right):
    return lax.dot_general(
        left, right, (((0,), (0,)), ((), ())), preferred_element_type=jnp.float32
    )


def local_kernel(
    factor,
    nz,
    rows_ref,
    gain_ref,
    gate_src,
    up_src,
    own_src,
    other_src,
    ahead_ref,
    behind_ref,
    far_ref,
    hub_ref,
    gate_own_ref,
    up_own_ref,
    normed_ref,
    grads_ref,
    gate_ref,
    up_ref,
    own_ref,
    other_ref,
    sems,
):
    copies = [
        pltpu.make_async_copy(src, dst, sems.at[at])
        for at, (src, dst) in enumerate(
            (
                (gate_src, gate_ref),
                (up_src, up_ref),
                (own_src, own_ref),
                (other_src, other_ref),
            )
        )
    ]
    for copy in copies:
        copy.start()
    z = lax.axis_index("z")
    half = lax.axis_index("yh")
    rows = own_ref.shape[1]
    width = own_ref.shape[0]
    scaled = normalize(rows_ref[...])[0]
    normed_ref[...] = (scaled * gain_ref[...]).astype(jnp.bfloat16)
    normed = normed_ref[...]
    copies[0].wait()
    gate_value = contract_last(normed, gate_ref[...])
    copies[1].wait()
    up_value = contract_last(normed, up_ref[...])
    copies[2].wait()
    copies[3].wait()
    own = own_ref[...].astype(jnp.float32).T
    other = other_ref[...].astype(jnp.float32).T
    first = half == 0
    upstream = jnp.concatenate(
        [jnp.where(first, own, other), jnp.where(first, other, own)], axis=0
    )
    sigmoid_gate = jax.nn.sigmoid(gate_value)
    weighted = upstream * sigmoid_gate
    grads_ref[:, width:] = (weighted * gate_value).astype(jnp.bfloat16)
    grads_ref[:, :width] = (
        weighted * up_value * (1.0 + gate_value * (1.0 - sigmoid_gate))
    ).astype(jnp.bfloat16)
    start = pl.multiple_of(half * rows, rows)
    gate_own_ref[...] = grads_ref[pl.ds(start, rows), :width]
    up_own_ref[...] = grads_ref[pl.ds(start, rows), width:]
    grads = grads_ref[...]
    depth = far_ref.shape[0]

    def block(relative):
        chunk = lax.rem(z - relative + 2 * nz, nz)
        lanes = pl.ds(pl.multiple_of(chunk * 2 * depth, 2 * depth), 2 * depth)
        both = contract_first(normed_ref[:, lanes], grads) * factor
        return jnp.where(first, both[:depth], both[depth:]).astype(jnp.bfloat16)

    for at, hub in enumerate(HUBS):
        ahead_ref[at] = block(hub - 1)
        behind_ref[at] = block(hub + 1)
    far_ref[...] = block(nz // 2)
    for at, hub in enumerate(HUBS):
        hub_ref[at] = block(hub)


def shift(value, hops, nz):
    return lax.ppermute(value, "z", [(i, (i + hops) % nz) for i in range(nz)])


def shards(residual, norm_gain, gate_weight, up_weight, hidden_grad):
    nz, nh, nt = lax.axis_size("z"), lax.axis_size("yh"), lax.axis_size(TENSOR)
    rows, width = hidden_grad.shape
    features = residual.shape[1]
    depth = features // (nz * nh)
    f32, bf16 = jnp.float32, jnp.bfloat16
    own = hidden_grad.T
    other = lax.ppermute(own, "yh", [(0, 1), (1, 0)])
    copies = jnp.broadcast_to(residual[None], (nh * nt,) + residual.shape)
    gathered = lax.all_to_all(copies, ("yh",) + TENSOR, 0, 0, tiled=True)
    gathered = gathered.reshape(nh * rows, features)
    factor = float(rows * nz * nh) ** (-0.5)
    shape = jax.ShapeDtypeStruct
    hubs = len(HUBS)
    ahead, behind, far, hub, gate_own, up_own = pl.pallas_call(
        functools.partial(local_kernel, factor, nz),
        out_shape=(
            shape((hubs, depth, 2 * width), bf16),
            shape((hubs, depth, 2 * width), bf16),
            shape((depth, 2 * width), bf16),
            shape((hubs, depth, 2 * width), bf16),
            shape((rows, width), bf16),
            shape((rows, width), bf16),
        ),
        in_specs=[pl.BlockSpec(memory_space=pltpu.VMEM)] * 2
        + [pl.BlockSpec(memory_space=pltpu.HBM)] * 4,
        scratch_shapes=[
            pltpu.VMEM((nh * rows, features), bf16),
            pltpu.VMEM((nh * rows, 2 * width), bf16),
            pltpu.VMEM((width, features), bf16),
            pltpu.VMEM((width, features), bf16),
            pltpu.VMEM((width, rows), bf16),
            pltpu.VMEM((width, rows), bf16),
            pltpu.SemaphoreType.DMA((4,)),
        ],
        compiler_params=pltpu.CompilerParams(vmem_limit_bytes=20 * 1024 * 1024),
        cost_estimate=pl.CostEstimate(
            flops=8 * nh * rows * features * width,
            bytes_accessed=8 * features * width,
            transcendentals=nh * rows * width,
        ),
        name="local",
    )(gathered, norm_gain.reshape(1, features), gate_weight.T, up_weight.T, own, other)

    from_far = shift(far, -2, nz)
    from_behind = shift(ahead, 1, nz)
    from_ahead = shift(behind, -1, nz)
    gate_own, up_own, from_far = lax.optimization_barrier((gate_own, up_own, from_far))

    part = (contract_last(gate_own, gate_weight) + contract_last(up_own, up_weight)).astype(bf16)
    blocks = part.reshape(nt, rows // nt, features)
    moved = lax.all_to_all(blocks, TENSOR, 0, 0, tiled=True)

    def joined(at):
        return (
            hub[at].astype(f32) + from_behind[at].astype(f32) + from_ahead[at].astype(f32)
        )

    plus, minus = lax.optimization_barrier(
        (joined(0).astype(bf16), (joined(4) + from_far.astype(f32)).astype(bf16))
    )
    plus, minus = lax.optimization_barrier((shift(plus, 3, nz), shift(minus, -3, nz)))
    plus, minus = lax.optimization_barrier(
        (
            (joined(1) + plus.astype(f32)).astype(bf16),
            (joined(3) + minus.astype(f32)).astype(bf16),
        )
    )
    plus, minus = shift(plus, 3, nz), shift(minus, -3, nz)
    total = (joined(2) + plus.astype(f32) + minus.astype(f32)).astype(bf16)

    scaled, inverse = normalize(residual)
    normed_grad = jnp.sum(moved.astype(f32), axis=0)
    weighted = normed_grad * norm_gain
    residual_grad = (
        (weighted - scaled * jnp.mean(weighted * scaled, axis=-1, keepdims=True)) * inverse
    ).astype(bf16)
    return (residual_grad, total[:, :width], total[:, width:])


def solution(mesh):
    fine = Mesh(mesh.devices.reshape(16, 2, 4, 2, 2), DP + TENSOR)
    return jax.shard_map(
        shards,
        mesh=fine,
        in_specs=(
            P(DP + TENSOR, None),
            P(),
            P(None, TENSOR),
            P(None, TENSOR),
            P(DP, TENSOR),
        ),
        out_specs=(P(DP + TENSOR, None), P(DP, TENSOR), P(DP, TENSOR)),
        check_vma=False,
    )
```

```python
import functools

import jax
import jax.numpy as jnp
from jax import lax
from jax.experimental import pallas as pl
from jax.experimental.pallas import tpu as pltpu
from jax.sharding import Mesh
from jax.sharding import PartitionSpec as P

EPSILON = 1e-05
DP = ("z", "yh")
TENSOR = ("x", "yl", "core")
OUTER = (-6, 6)
INNER = (-3, 0, 3)


def normalize(residual):
    values = residual.astype(jnp.float32)
    inverse = lax.rsqrt(jnp.mean(values * values, axis=-1, keepdims=True) + EPSILON)
    return (values * inverse, inverse)


def contract_last(left, right):
    return lax.dot_general(
        left, right, (((1,), (1,)), ((), ())), preferred_element_type=jnp.float32
    )


def contract_first(left, right):
    return lax.dot_general(
        left, right, (((0,), (0,)), ((), ())), preferred_element_type=jnp.float32
    )


def local_kernel(
    factor,
    nz,
    rows_ref,
    gain_ref,
    weight_ref,
    own_ref,
    other_ref,
    far_ref,
    outer_ahead_ref,
    outer_behind_ref,
    inner_ahead_ref,
    inner_behind_ref,
    hub_ref,
    grads_own_ref,
    normed_ref,
    grads_ref,
):
    z = lax.axis_index("z")
    half = lax.axis_index("yh")
    rows, width = own_ref.shape
    scaled = normalize(rows_ref[...])[0]
    normed_ref[...] = (scaled * gain_ref[...]).astype(jnp.bfloat16)
    normed = normed_ref[...]
    gate_value = contract_last(normed, weight_ref[:width])
    up_value = contract_last(normed, weight_ref[width:])
    own = own_ref[...].astype(jnp.float32)
    other = other_ref[...].astype(jnp.float32)
    first = half == 0
    upstream = jnp.concatenate(
        [jnp.where(first, own, other), jnp.where(first, other, own)], axis=0
    )
    sigmoid_gate = jax.nn.sigmoid(gate_value)
    weighted = upstream * sigmoid_gate
    grads_ref[:, width:] = (weighted * gate_value).astype(jnp.bfloat16)
    grads_ref[:, :width] = (
        weighted * up_value * (1.0 + gate_value * (1.0 - sigmoid_gate))
    ).astype(jnp.bfloat16)
    start = pl.multiple_of(half * rows, rows)
    grads_own_ref[...] = grads_ref[pl.ds(start, rows), :]
    grads = grads_ref[...]
    depth = far_ref.shape[0]

    def block(relative):
        chunk = lax.rem(z - relative + 2 * nz, nz)
        lanes = pl.ds(pl.multiple_of(chunk * 2 * depth, 2 * depth), 2 * depth)
        both = contract_first(normed_ref[:, lanes], grads) * factor
        return jnp.where(first, both[:depth], both[depth:]).astype(jnp.bfloat16)

    far_ref[...] = block(nz // 2)
    for at, hub in enumerate(OUTER):
        outer_ahead_ref[at] = block(hub - 1)
        outer_behind_ref[at] = block(hub + 1)
    for at, hub in enumerate(INNER):
        inner_ahead_ref[at] = block(hub - 1)
        inner_behind_ref[at] = block(hub + 1)
    for at, hub in enumerate(OUTER + INNER):
        hub_ref[at] = block(hub)


def shift(value, hops, nz):
    return lax.ppermute(value, "z", [(i, (i + hops) % nz) for i in range(nz)])


def shards(residual, norm_gain, gate_weight, up_weight, hidden_grad):
    nz, nh, nt = lax.axis_size("z"), lax.axis_size("yh"), lax.axis_size(TENSOR)
    rows, width = hidden_grad.shape
    features = residual.shape[1]
    depth = features // (nz * nh)
    f32, bf16 = jnp.float32, jnp.bfloat16
    weight = jnp.concatenate([gate_weight.T, up_weight.T], axis=0)
    own = hidden_grad
    other = lax.ppermute(own, "yh", [(0, 1), (1, 0)])
    copies = jnp.broadcast_to(residual[None], (nh * nt,) + residual.shape)
    gathered = lax.all_to_all(copies, ("yh",) + TENSOR, 0, 0, tiled=True)
    gathered = gathered.reshape(nh * rows, features)
    factor = float(rows * nz * nh) ** (-0.5)
    shape = jax.ShapeDtypeStruct
    far, outer_ahead, outer_behind, inner_ahead, inner_behind, hub, grads_own = pl.pallas_call(
        functools.partial(local_kernel, factor, nz),
        out_shape=(
            shape((depth, 2 * width), bf16),
            shape((len(OUTER), depth, 2 * width), bf16),
            shape((len(OUTER), depth, 2 * width), bf16),
            shape((len(INNER), depth, 2 * width), bf16),
            shape((len(INNER), depth, 2 * width), bf16),
            shape((len(OUTER + INNER), depth, 2 * width), bf16),
            shape((rows, 2 * width), bf16),
        ),
        scratch_shapes=[
            pltpu.VMEM((nh * rows, features), bf16),
            pltpu.VMEM((nh * rows, 2 * width), bf16),
        ],
        compiler_params=pltpu.CompilerParams(vmem_limit_bytes=20 * 1024 * 1024),
        cost_estimate=pl.CostEstimate(
            flops=8 * nh * rows * features * width,
            bytes_accessed=8 * features * width,
            transcendentals=nh * rows * width,
        ),
        name="local",
    )(gathered, norm_gain.reshape(1, features), weight, own, other)

    from_far = shift(far, -2, nz).astype(f32)
    outer_ahead, outer_behind = shift(outer_ahead, 1, nz), shift(outer_behind, -1, nz)
    inner_ahead, inner_behind = shift(inner_ahead, 1, nz), shift(inner_behind, -1, nz)
    hub = hub.astype(f32)
    outer = hub[:2] + outer_ahead.astype(f32) + outer_behind.astype(f32)
    plus, minus = lax.optimization_barrier(
        (outer[0].astype(bf16), (outer[1] + from_far).astype(bf16))
    )
    grads_own, first_sum = lax.optimization_barrier((grads_own, plus))
    plus, minus = shift(first_sum, 3, nz), shift(minus, -3, nz)

    part = jnp.dot(grads_own, weight, preferred_element_type=f32).astype(bf16)
    blocks = part.reshape(nt, rows // nt, features)
    moved = lax.all_to_all(blocks, TENSOR, 0, 0, tiled=True)

    inner = hub[2:] + inner_ahead.astype(f32) + inner_behind.astype(f32)
    plus, minus = lax.optimization_barrier((plus, minus))
    plus, minus = lax.optimization_barrier(
        (
            (inner[0] + plus.astype(f32)).astype(bf16),
            (inner[2] + minus.astype(f32)).astype(bf16),
        )
    )
    plus, minus = shift(plus, 3, nz), shift(minus, -3, nz)
    total = (inner[1] + plus.astype(f32) + minus.astype(f32)).astype(bf16)

    scaled, inverse = normalize(residual)
    normed_grad = jnp.sum(moved.astype(f32), axis=0)
    weighted = normed_grad * norm_gain
    residual_grad = (
        (weighted - scaled * jnp.mean(weighted * scaled, axis=-1, keepdims=True)) * inverse
    ).astype(bf16)
    return (residual_grad, total[:, :width], total[:, width:])


def solution(mesh):
    fine = Mesh(mesh.devices.reshape(16, 2, 4, 2, 2), DP + TENSOR)
    return jax.shard_map(
        shards,
        mesh=fine,
        in_specs=(
            P(DP + TENSOR, None),
            P(),
            P(None, TENSOR),
            P(None, TENSOR),
            P(DP, TENSOR),
        ),
        out_specs=(P(DP + TENSOR, None), P(DP, TENSOR), P(DP, TENSOR)),
        check_vma=False,
    )
```

```python
import functools

import jax
import jax.numpy as jnp
from jax import lax
from jax.experimental import pallas as pl
from jax.experimental.pallas import tpu as pltpu
from jax.sharding import Mesh
from jax.sharding import PartitionSpec as P

EPSILON = 1e-05
DP = ("z", "yh")
TENSOR = ("x", "yl", "core")
OUTER = (-6, 6)
INNER = (-3, 0, 3)


def normalize(residual):
    values = residual.astype(jnp.float32)
    inverse = lax.rsqrt(jnp.mean(values * values, axis=-1, keepdims=True) + EPSILON)
    return (values * inverse, inverse)


def contract_last(left, right):
    return lax.dot_general(
        left, right, (((1,), (1,)), ((), ())), preferred_element_type=jnp.float32
    )


def contract_first(left, right):
    return lax.dot_general(
        left, right, (((0,), (0,)), ((), ())), preferred_element_type=jnp.float32
    )


def local_kernel(
    factor,
    nz,
    rows_ref,
    gain_ref,
    weight_ref,
    own_ref,
    other_ref,
    far_ref,
    outer_ahead_ref,
    outer_behind_ref,
    inner_ahead_ref,
    inner_behind_ref,
    hub_ref,
    grads_own_ref,
    normed_ref,
    grads_ref,
):
    z = lax.axis_index("z")
    half = lax.axis_index("yh")
    rows, width = own_ref.shape
    scaled = normalize(rows_ref[...])[0]
    normed_ref[...] = (scaled * gain_ref[...]).astype(jnp.bfloat16)
    normed = normed_ref[...]
    gate_value = contract_last(normed, weight_ref[:width])
    up_value = contract_last(normed, weight_ref[width:])
    own = own_ref[...].astype(jnp.float32)
    other = other_ref[...].astype(jnp.float32)
    first = half == 0
    upstream = jnp.concatenate(
        [jnp.where(first, own, other), jnp.where(first, other, own)], axis=0
    )
    sigmoid_gate = jax.nn.sigmoid(gate_value)
    weighted = upstream * sigmoid_gate
    grads_ref[:, width:] = (weighted * gate_value).astype(jnp.bfloat16)
    grads_ref[:, :width] = (
        weighted * up_value * (1.0 + gate_value * (1.0 - sigmoid_gate))
    ).astype(jnp.bfloat16)
    start = pl.multiple_of(half * rows, rows)
    grads_own_ref[...] = grads_ref[pl.ds(start, rows), :]
    grads = grads_ref[...]
    depth = far_ref.shape[0]

    sign = 1 - 2 * lax.rem(z, 2)

    def block(relative):
        chunk = lax.rem(z - sign * relative + 2 * nz, nz)
        lanes = pl.ds(pl.multiple_of(chunk * 2 * depth, 2 * depth), 2 * depth)
        both = contract_first(normed_ref[:, lanes], grads) * factor
        return jnp.where(first, both[:depth], both[depth:]).astype(jnp.bfloat16)

    far_ref[...] = block(nz // 2)
    for at, hub in enumerate(OUTER):
        outer_ahead_ref[at] = block(-hub - 1)
        outer_behind_ref[at] = block(-hub + 1)
    for at, hub in enumerate(INNER):
        inner_ahead_ref[at] = block(-hub - 1)
        inner_behind_ref[at] = block(-hub + 1)
    for at, hub in enumerate(OUTER + INNER):
        hub_ref[at] = block(hub)


def join_kernel(gate_ref, up_ref, both_ref):
    width = gate_ref.shape[0]
    both_ref[:width] = gate_ref[...]
    both_ref[width:] = up_ref[...]


def move(value, hops, nz):
    pairs = [(i, (i + (1 - 2 * (i % 2)) * hops) % nz) for i in range(nz)]
    return lax.ppermute(value, "z", pairs)


def shards(residual, norm_gain, gate_weight, up_weight, hidden_grad):
    nz, nh, nt = lax.axis_size("z"), lax.axis_size("yh"), lax.axis_size(TENSOR)
    rows, width = hidden_grad.shape
    features = residual.shape[1]
    depth = features // (nz * nh)
    f32, bf16 = jnp.float32, jnp.bfloat16
    weight = pl.pallas_call(
        join_kernel,
        out_shape=jax.ShapeDtypeStruct((2 * width, features), bf16),
        compiler_params=pltpu.CompilerParams(vmem_limit_bytes=20 * 1024 * 1024),
        name="join",
    )(gate_weight.T, up_weight.T)
    own = hidden_grad
    other = lax.ppermute(own, "yh", [(0, 1), (1, 0)])
    copies = jnp.broadcast_to(residual[None], (nh * nt,) + residual.shape)
    gathered = lax.all_to_all(copies, ("yh",) + TENSOR, 0, 0, tiled=True)
    gathered = gathered.reshape(nh * rows, features)
    factor = float(rows * nz * nh) ** (-0.5)
    shape = jax.ShapeDtypeStruct
    far, outer_ahead, outer_behind, inner_ahead, inner_behind, hub, grads_own = pl.pallas_call(
        functools.partial(local_kernel, factor, nz),
        out_shape=(
            shape((depth, 2 * width), bf16),
            shape((len(OUTER), depth, 2 * width), bf16),
            shape((len(OUTER), depth, 2 * width), bf16),
            shape((len(INNER), depth, 2 * width), bf16),
            shape((len(INNER), depth, 2 * width), bf16),
            shape((len(OUTER + INNER), depth, 2 * width), bf16),
            shape((rows, 2 * width), bf16),
        ),
        scratch_shapes=[
            pltpu.VMEM((nh * rows, features), bf16),
            pltpu.VMEM((nh * rows, 2 * width), bf16),
        ],
        compiler_params=pltpu.CompilerParams(vmem_limit_bytes=20 * 1024 * 1024),
        cost_estimate=pl.CostEstimate(
            flops=8 * nh * rows * features * width,
            bytes_accessed=8 * features * width,
            transcendentals=nh * rows * width,
        ),
        name="local",
    )(gathered, norm_gain.reshape(1, features), weight, own, other)

    from_far = move(far, -2, nz).astype(f32)
    outer_ahead, outer_behind = move(outer_ahead, 1, nz), move(outer_behind, -1, nz)
    inner_ahead, inner_behind = move(inner_ahead, 1, nz), move(inner_behind, -1, nz)
    hub = hub.astype(f32)
    outer = hub[:2] + outer_ahead.astype(f32) + outer_behind.astype(f32)
    plus, minus = lax.optimization_barrier(
        (outer[0].astype(bf16), (outer[1] + from_far).astype(bf16))
    )
    grads_own, first_sum = lax.optimization_barrier((grads_own, plus))
    plus, minus = move(first_sum, 3, nz), move(minus, -3, nz)

    part = jnp.dot(grads_own, weight, preferred_element_type=f32).astype(bf16)
    blocks = part.reshape(nt, rows // nt, features)
    moved = lax.all_to_all(blocks, TENSOR, 0, 0, tiled=True)

    inner = hub[2:] + inner_ahead.astype(f32) + inner_behind.astype(f32)
    plus, minus = lax.optimization_barrier((plus, minus))
    plus, minus = lax.optimization_barrier(
        (
            (inner[0] + minus.astype(f32)).astype(bf16),
            (inner[2] + plus.astype(f32)).astype(bf16),
        )
    )
    plus, minus = move(plus, 3, nz), move(minus, -3, nz)

    scaled, inverse = normalize(residual)
    normed_grad = jnp.sum(moved.astype(f32), axis=0)
    weighted = normed_grad * norm_gain
    residual_grad = (
        (weighted - scaled * jnp.mean(weighted * scaled, axis=-1, keepdims=True)) * inverse
    ).astype(bf16)
    total = (inner[1] + plus.astype(f32) + minus.astype(f32)).astype(bf16)
    return (residual_grad, total[:, :width], total[:, width:])


def solution(mesh):
    fine = Mesh(mesh.devices.reshape(16, 2, 4, 2, 2), DP + TENSOR)
    return jax.shard_map(
        shards,
        mesh=fine,
        in_specs=(
            P(DP + TENSOR, None),
            P(),
            P(None, TENSOR),
            P(None, TENSOR),
            P(DP, TENSOR),
        ),
        out_specs=(P(DP + TENSOR, None), P(DP, TENSOR), P(DP, TENSOR)),
        check_vma=False,
    )
```

```python
import functools

import jax
import jax.numpy as jnp
from jax import lax
from jax.experimental import pallas as pl
from jax.experimental.pallas import tpu as pltpu
from jax.sharding import Mesh
from jax.sharding import PartitionSpec as P

EPSILON = 1e-05
DP = ("z", "yh")
TENSOR = ("x", "yl", "core")
OUTER = (-6, 6)
INNER = (-3, 0, 3)


def normalize(residual):
    values = residual.astype(jnp.float32)
    inverse = lax.rsqrt(jnp.mean(values * values, axis=-1, keepdims=True) + EPSILON)
    return (values * inverse, inverse)


def contract_last(left, right):
    return lax.dot_general(
        left, right, (((1,), (1,)), ((), ())), preferred_element_type=jnp.float32
    )


def contract_first(left, right):
    return lax.dot_general(
        left, right, (((0,), (0,)), ((), ())), preferred_element_type=jnp.float32
    )


def local_kernel(
    factor,
    nz,
    block_rows,
    same_ref,
    swapped_ref,
    gain_ref,
    gate_ref,
    up_ref,
    own_ref,
    other_ref,
    far_ref,
    outer_ahead_ref,
    outer_behind_ref,
    inner_ahead_ref,
    inner_behind_ref,
    outer_hub_ref,
    inner_hub_ref,
    grads_own_ref,
    normed_ref,
    grads_ref,
):
    z = lax.axis_index("z")
    half = lax.axis_index("yh")
    rows, width = own_ref.shape
    tokens = same_ref.shape[0]
    gain = gain_ref[...]
    normed_ref[:tokens] = (normalize(same_ref[...])[0] * gain).astype(jnp.bfloat16)
    normed_ref[tokens:] = (normalize(swapped_ref[...])[0] * gain).astype(jnp.bfloat16)
    normed = normed_ref[...]
    gate_value = contract_last(normed, gate_ref[...])
    up_value = contract_last(normed, up_ref[...])
    first = half == 0
    even = lax.axis_index("core") == 0
    count = lax.axis_size("core")
    split = (rows // (count * block_rows), count, block_rows, width)
    own = own_ref[...].astype(jnp.float32).reshape(split)
    other = other_ref[...].astype(jnp.float32).reshape(split)

    def by_core(values, same):
        near, away = (0, 1) if same else (1, 0)
        return jnp.where(even, values[:, near], values[:, away]).reshape(rows // count, width)

    pieces = []
    for same in (True, False):
        mine, theirs = by_core(own, same), by_core(other, same)
        pieces += [jnp.where(first, mine, theirs), jnp.where(first, theirs, mine)]
    upstream = jnp.concatenate(pieces, axis=0)
    sigmoid_gate = jax.nn.sigmoid(gate_value)
    weighted = upstream * sigmoid_gate
    gate_grad = weighted * up_value * (1.0 + gate_value * (1.0 - sigmoid_gate))
    up_grad = weighted * gate_value
    grads_ref[:, :width] = gate_grad.astype(jnp.bfloat16)
    grads_ref[:, width:] = up_grad.astype(jnp.bfloat16)
    piece = rows // count

    def own_rows(values):
        near = jnp.where(first, values[:piece], values[piece : 2 * piece])
        away = jnp.where(first, values[2 * piece : 3 * piece], values[3 * piece :])
        near = near.reshape(piece // block_rows, 1, block_rows, width)
        away = away.reshape(piece // block_rows, 1, block_rows, width)
        both = jnp.concatenate(
            [jnp.where(even, near, away), jnp.where(even, away, near)], axis=1
        )
        return both.reshape(rows, width).astype(jnp.bfloat16)

    grads_own_ref[:, :width] = own_rows(gate_grad)
    grads_own_ref[:, width:] = own_rows(up_grad)
    grads = grads_ref[...]
    depth = far_ref.shape[0]

    sign = 1 - 2 * lax.rem(z, 2)

    def block(relative):
        chunk = lax.rem(z - sign * relative + 2 * nz, nz)
        lanes = pl.ds(pl.multiple_of(chunk * 2 * depth, 2 * depth), 2 * depth)
        both = contract_first(normed_ref[:, lanes], grads) * factor
        return jnp.where(first, both[:depth], both[depth:]).astype(jnp.bfloat16)

    far_ref[...] = block(nz // 2)
    for at, hub in enumerate(OUTER):
        outer_ahead_ref[at] = block(-hub - 1)
        outer_behind_ref[at] = block(-hub + 1)
    for at, hub in enumerate(INNER):
        inner_ahead_ref[at] = block(-hub - 1)
        inner_behind_ref[at] = block(-hub + 1)
    for at, hub in enumerate(OUTER):
        outer_hub_ref[at] = block(hub)
    for at, hub in enumerate(INNER):
        inner_hub_ref[at] = block(hub)


def move(value, hops, nz):
    pairs = [(i, (i + (1 - 2 * (i % 2)) * hops) % nz) for i in range(nz)]
    return lax.ppermute(value, "z", pairs)


def shards(residual, norm_gain, gate_weight, up_weight, hidden_grad):
    nz, nh, nt = lax.axis_size("z"), lax.axis_size("yh"), lax.axis_size(TENSOR)
    rows, width = hidden_grad.shape
    features = residual.shape[1]
    depth = features // (nz * nh)
    f32, bf16 = jnp.float32, jnp.bfloat16
    own = hidden_grad
    other = lax.ppermute(own, "yh", [(0, 1), (1, 0)])
    chips = nh * nt // lax.axis_size("core")
    copies = jnp.broadcast_to(residual[None], (chips,) + residual.shape)
    same = lax.all_to_all(copies, ("yh", "x", "yl"), 0, 0, tiled=True)
    same = same.reshape(chips * residual.shape[0], features)
    same, other = lax.optimization_barrier((same, other))
    swapped = lax.ppermute(same, "core", [(0, 1), (1, 0)])
    factor = float(rows * nz * nh) ** (-0.5)
    shape = jax.ShapeDtypeStruct
    far, outer_ahead, outer_behind, inner_ahead, inner_behind, outer_hub, inner_hub, grads_own = pl.pallas_call(
        functools.partial(local_kernel, factor, nz, residual.shape[0]),
        out_shape=(
            shape((depth, 2 * width), bf16),
            shape((len(OUTER), depth, 2 * width), bf16),
            shape((len(OUTER), depth, 2 * width), bf16),
            shape((len(INNER), depth, 2 * width), bf16),
            shape((len(INNER), depth, 2 * width), bf16),
            shape((len(OUTER), depth, 2 * width), bf16),
            shape((len(INNER), depth, 2 * width), bf16),
            shape((rows, 2 * width), bf16),
        ),
        scratch_shapes=[
            pltpu.VMEM((nh * rows, features), bf16),
            pltpu.VMEM((nh * rows, 2 * width), bf16),
        ],
        compiler_params=pltpu.CompilerParams(vmem_limit_bytes=20 * 1024 * 1024),
        cost_estimate=pl.CostEstimate(
            flops=8 * nh * rows * features * width,
            bytes_accessed=8 * features * width,
            transcendentals=nh * rows * width,
        ),
        name="local",
    )(same, swapped, norm_gain.reshape(1, features), gate_weight.T, up_weight.T, own, other)

    from_far = move(far, -2, nz).astype(f32)
    outer_ahead, outer_behind = move(outer_ahead, 1, nz), move(outer_behind, -1, nz)
    inner_ahead, inner_behind = move(inner_ahead, 1, nz), move(inner_behind, -1, nz)

    def outer(at):
        return (
            outer_hub[at].astype(f32)
            + outer_ahead[at].astype(f32)
            + outer_behind[at].astype(f32)
        )

    def inner(at):
        return (
            inner_hub[at].astype(f32)
            + inner_ahead[at].astype(f32)
            + inner_behind[at].astype(f32)
        )

    plus, minus = lax.optimization_barrier(
        (outer(0).astype(bf16), (outer(1) + from_far).astype(bf16))
    )
    grads_own, first_sum = lax.optimization_barrier((grads_own, plus))
    plus, minus = move(first_sum, 3, nz), move(minus, -3, nz)

    part = contract_last(grads_own[:, :width], gate_weight)
    part = (part + contract_last(grads_own[:, width:], up_weight)).astype(bf16)
    blocks = part.reshape(nt, rows // nt, features)
    moved = lax.all_to_all(blocks, TENSOR, 0, 0, tiled=True)

    plus, minus = lax.optimization_barrier((plus, minus))
    plus, minus = lax.optimization_barrier(
        (
            (inner(0) + minus.astype(f32)).astype(bf16),
            (inner(2) + plus.astype(f32)).astype(bf16),
        )
    )
    plus, minus = move(plus, 3, nz), move(minus, -3, nz)

    scaled, inverse = normalize(residual)
    normed_grad = jnp.sum(moved.astype(f32), axis=0)
    weighted = normed_grad * norm_gain
    residual_grad = (
        (weighted - scaled * jnp.mean(weighted * scaled, axis=-1, keepdims=True)) * inverse
    ).astype(bf16)
    total = (inner(1) + plus.astype(f32) + minus.astype(f32)).astype(bf16)
    return (residual_grad, total[:, :width], total[:, width:])


def solution(mesh):
    fine = Mesh(mesh.devices.reshape(16, 2, 4, 2, 2), DP + TENSOR)
    return jax.shard_map(
        shards,
        mesh=fine,
        in_specs=(
            P(DP + TENSOR, None),
            P(),
            P(None, TENSOR),
            P(None, TENSOR),
            P(DP, TENSOR),
        ),
        out_specs=(P(DP + TENSOR, None), P(DP, TENSOR), P(DP, TENSOR)),
        check_vma=False,
    )
```

```python
import functools

import jax
import jax.numpy as jnp
from jax import lax
from jax.experimental import pallas as pl
from jax.experimental.pallas import tpu as pltpu
from jax.sharding import Mesh
from jax.sharding import PartitionSpec as P

EPSILON = 1e-05
DP = ("z", "yh")
TENSOR = ("x", "yl", "core")
HUBS = (-6, 6, -3, 0, 3)


def normalize(residual):
    values = residual.astype(jnp.float32)
    inverse = lax.rsqrt(jnp.mean(values * values, axis=-1, keepdims=True) + EPSILON)
    return (values * inverse, inverse)


def contract_last(left, right):
    return lax.dot_general(
        left, right, (((1,), (1,)), ((), ())), preferred_element_type=jnp.float32
    )


def contract_first(left, right):
    return lax.dot_general(
        left, right, (((0,), (0,)), ((), ())), preferred_element_type=jnp.float32
    )


def local_kernel(
    factor,
    nz,
    block_rows,
    same_ref,
    swapped_ref,
    gain_ref,
    gate_ref,
    up_ref,
    own_ref,
    other_ref,
    far_ref,
    ahead_ref,
    behind_ref,
    hub_ref,
    grads_own_ref,
    normed_ref,
    grads_ref,
):
    z = lax.axis_index("z")
    half = lax.axis_index("yh")
    rows, width = own_ref.shape
    tokens = same_ref.shape[0]
    gain = gain_ref[...]
    normed_ref[:tokens] = (normalize(same_ref[...])[0] * gain).astype(jnp.bfloat16)
    normed_ref[tokens:] = (normalize(swapped_ref[...])[0] * gain).astype(jnp.bfloat16)
    normed = normed_ref[...]
    gate_value = contract_last(normed, gate_ref[...])
    up_value = contract_last(normed, up_ref[...])
    first = half == 0
    even = lax.axis_index("core") == 0
    count = lax.axis_size("core")
    split = (rows // (count * block_rows), count, block_rows, width)
    own = own_ref[...].astype(jnp.float32).reshape(split)
    other = other_ref[...].astype(jnp.float32).reshape(split)

    def by_core(values, same):
        near, away = (0, 1) if same else (1, 0)
        return jnp.where(even, values[:, near], values[:, away]).reshape(rows // count, width)

    pieces = []
    for same in (True, False):
        mine, theirs = by_core(own, same), by_core(other, same)
        pieces += [jnp.where(first, mine, theirs), jnp.where(first, theirs, mine)]
    upstream = jnp.concatenate(pieces, axis=0)
    sigmoid_gate = jax.nn.sigmoid(gate_value)
    weighted = upstream * sigmoid_gate
    gate_grad = weighted * up_value * (1.0 + gate_value * (1.0 - sigmoid_gate))
    up_grad = weighted * gate_value
    grads_ref[:, :width] = gate_grad.astype(jnp.bfloat16)
    grads_ref[:, width:] = up_grad.astype(jnp.bfloat16)
    piece = rows // count

    def own_rows(values):
        near = jnp.where(first, values[:piece], values[piece : 2 * piece])
        away = jnp.where(first, values[2 * piece : 3 * piece], values[3 * piece :])
        near = near.reshape(piece // block_rows, 1, block_rows, width)
        away = away.reshape(piece // block_rows, 1, block_rows, width)
        both = jnp.concatenate(
            [jnp.where(even, near, away), jnp.where(even, away, near)], axis=1
        )
        return both.reshape(rows, width).astype(jnp.bfloat16)

    grads_own_ref[:, :width] = own_rows(gate_grad)
    grads_own_ref[:, width:] = own_rows(up_grad)
    grads = grads_ref[...]
    depth = far_ref.shape[0]

    sign = 1 - 2 * lax.rem(z, 2)

    def block(relative):
        chunk = lax.rem(z - sign * relative + 2 * nz, nz)
        lanes = pl.ds(pl.multiple_of(chunk * 2 * depth, 2 * depth), 2 * depth)
        both = contract_first(normed_ref[:, lanes], grads) * factor
        return jnp.where(first, both[:depth], both[depth:]).astype(jnp.bfloat16)

    far_ref[...] = block(nz // 2)
    for at, hub in enumerate(HUBS):
        ahead_ref[at] = block(-hub - 1)
        behind_ref[at] = block(-hub + 1)
        hub_ref[at] = block(hub)


def move(value, hops, nz):
    pairs = [(i, (i + (1 - 2 * (i % 2)) * hops) % nz) for i in range(nz)]
    return lax.ppermute(value, "z", pairs)


def shards(residual, norm_gain, gate_weight, up_weight, hidden_grad):
    nz, nh, nt = lax.axis_size("z"), lax.axis_size("yh"), lax.axis_size(TENSOR)
    rows, width = hidden_grad.shape
    features = residual.shape[1]
    depth = features // (nz * nh)
    f32, bf16 = jnp.float32, jnp.bfloat16
    own = hidden_grad
    other = lax.ppermute(own, "yh", [(0, 1), (1, 0)])
    chips = nh * nt // lax.axis_size("core")
    copies = jnp.broadcast_to(residual[None], (chips,) + residual.shape)
    same = lax.all_to_all(copies, ("yh", "x", "yl"), 0, 0, tiled=True)
    same = same.reshape(chips * residual.shape[0], features)
    same, other = lax.optimization_barrier((same, other))
    swapped = lax.ppermute(same, "core", [(0, 1), (1, 0)])
    factor = float(rows * nz * nh) ** (-0.5)
    shape = jax.ShapeDtypeStruct
    far, ahead, behind, hub, grads_own = pl.pallas_call(
        functools.partial(local_kernel, factor, nz, residual.shape[0]),
        out_shape=(
            shape((depth, 2 * width), bf16),
            shape((len(HUBS), depth, 2 * width), bf16),
            shape((len(HUBS), depth, 2 * width), bf16),
            shape((len(HUBS), depth, 2 * width), bf16),
            shape((rows, 2 * width), bf16),
        ),
        scratch_shapes=[
            pltpu.VMEM((nh * rows, features), bf16),
            pltpu.VMEM((nh * rows, 2 * width), bf16),
        ],
        compiler_params=pltpu.CompilerParams(vmem_limit_bytes=20 * 1024 * 1024),
        cost_estimate=pl.CostEstimate(
            flops=8 * nh * rows * features * width,
            bytes_accessed=8 * features * width,
            transcendentals=nh * rows * width,
        ),
        name="local",
    )(same, swapped, norm_gain.reshape(1, features), gate_weight.T, up_weight.T, own, other)

    from_far = move(far, -2, nz)
    ahead, behind = move(ahead, 1, nz), move(behind, -1, nz)
    grads_own, from_far = lax.optimization_barrier((grads_own, from_far))

    part = contract_last(grads_own[:, :width], gate_weight)
    part = (part + contract_last(grads_own[:, width:], up_weight)).astype(bf16)
    blocks = part.reshape(nt, rows // nt, features)
    moved = lax.all_to_all(blocks, TENSOR, 0, 0, tiled=True)

    def joined(at):
        return hub[at].astype(f32) + ahead[at].astype(f32) + behind[at].astype(f32)

    plus, minus = lax.optimization_barrier(
        (joined(0).astype(bf16), (joined(1) + from_far.astype(f32)).astype(bf16))
    )
    plus, minus = move(plus, 3, nz), move(minus, -3, nz)
    plus, minus = lax.optimization_barrier((plus, minus))
    plus, minus = lax.optimization_barrier(
        (
            (joined(2) + minus.astype(f32)).astype(bf16),
            (joined(4) + plus.astype(f32)).astype(bf16),
        )
    )
    plus, minus = move(plus, 3, nz), move(minus, -3, nz)
    total = (joined(3) + plus.astype(f32) + minus.astype(f32)).astype(bf16)

    scaled, inverse = normalize(residual)
    normed_grad = jnp.sum(moved.astype(f32), axis=0)
    weighted = normed_grad * norm_gain
    residual_grad = (
        (weighted - scaled * jnp.mean(weighted * scaled, axis=-1, keepdims=True)) * inverse
    ).astype(bf16)
    return (residual_grad, total[:, :width], total[:, width:])


def solution(mesh):
    fine = Mesh(mesh.devices.reshape(16, 2, 4, 2, 2), DP + TENSOR)
    return jax.shard_map(
        shards,
        mesh=fine,
        in_specs=(
            P(DP + TENSOR, None),
            P(),
            P(None, TENSOR),
            P(None, TENSOR),
            P(DP, TENSOR),
        ),
        out_specs=(P(DP + TENSOR, None), P(DP, TENSOR), P(DP, TENSOR)),
        check_vma=False,
    )
```

```python
import functools

import jax
import jax.numpy as jnp
from jax import lax
from jax.experimental import pallas as pl
from jax.experimental.pallas import tpu as pltpu
from jax.sharding import Mesh
from jax.sharding import PartitionSpec as P

EPSILON = 1e-05
DP = ("z", "yh")
TENSOR = ("x", "yl", "core")
HUBS = (3, -3, 0)
LOWER = (0, 2)


def normalize(residual):
    values = residual.astype(jnp.float32)
    inverse = lax.rsqrt(jnp.mean(values * values, axis=-1, keepdims=True) + EPSILON)
    return (values * inverse, inverse)


def contract_last(left, right):
    return lax.dot_general(
        left, right, (((1,), (1,)), ((), ())), preferred_element_type=jnp.float32
    )


def contract_first(left, right):
    return lax.dot_general(
        left, right, (((0,), (0,)), ((), ())), preferred_element_type=jnp.float32
    )


def local_kernel(
    factor,
    nz,
    block_rows,
    same_ref,
    swapped_ref,
    gain_ref,
    gate_ref,
    up_ref,
    own_ref,
    other_ref,
    ahead_ref,
    behind_ref,
    hub_ref,
    grads_own_ref,
    normed_ref,
    grads_ref,
):
    z = lax.axis_index("z")
    half = lax.axis_index("yh")
    planes, rows, width = own_ref.shape
    tokens = same_ref.shape[0]
    gain = gain_ref[...]
    normed_ref[:tokens] = (normalize(same_ref[...])[0] * gain).astype(jnp.bfloat16)
    normed_ref[tokens:] = (normalize(swapped_ref[...])[0] * gain).astype(jnp.bfloat16)
    normed = normed_ref[...]
    gate_value = contract_last(normed, gate_ref[...])
    up_value = contract_last(normed, up_ref[...])
    first = half == 0
    even = lax.axis_index("core") == 0
    count = lax.axis_size("core")
    split = (planes, rows // (count * block_rows), count, block_rows, width)
    own = own_ref[...].astype(jnp.float32).reshape(split)
    other = other_ref[...].astype(jnp.float32).reshape(split)
    piece = planes * rows // count

    def by_core(values, same):
        near, away = (0, 1) if same else (1, 0)
        chosen = jnp.where(even, values[:, :, near], values[:, :, away])
        return jnp.stack([chosen[at] for at in range(planes)], axis=1).reshape(piece, width)

    pieces = []
    for same in (True, False):
        mine, theirs = by_core(own, same), by_core(other, same)
        pieces += [jnp.where(first, mine, theirs), jnp.where(first, theirs, mine)]
    upstream = jnp.concatenate(pieces, axis=0)
    sigmoid_gate = jax.nn.sigmoid(gate_value)
    weighted = upstream * sigmoid_gate
    gate_grad = weighted * up_value * (1.0 + gate_value * (1.0 - sigmoid_gate))
    up_grad = weighted * gate_value
    grads_ref[:, :width] = gate_grad.astype(jnp.bfloat16)
    grads_ref[:, width:] = up_grad.astype(jnp.bfloat16)

    def own_rows(values):
        near = jnp.where(first, values[:piece], values[piece : 2 * piece])
        away = jnp.where(first, values[2 * piece : 3 * piece], values[3 * piece :])
        shape = (piece // (planes * block_rows), planes, block_rows, width)
        near, away = near.reshape(shape)[:, :1], away.reshape(shape)[:, :1]
        both = jnp.concatenate(
            [jnp.where(even, near, away), jnp.where(even, away, near)], axis=1
        )
        return both.reshape(rows, width).astype(jnp.bfloat16)

    grads_own_ref[:, :width] = own_rows(gate_grad)
    grads_own_ref[:, width:] = own_rows(up_grad)
    grads = grads_ref[...]
    depth = hub_ref.shape[1]
    pair, parity = z // planes, lax.rem(z, planes)
    pairs = nz // planes

    sign = 1 - 2 * lax.rem(pair, 2)

    def block(relative):
        chunk = lax.rem(pair - sign * relative + 2 * pairs, pairs) * planes + parity
        lanes = pl.ds(pl.multiple_of(chunk * 2 * depth, 2 * depth), 2 * depth)
        both = contract_first(normed_ref[:, lanes], grads) * factor
        return jnp.where(first, both[:depth], both[depth:]).astype(jnp.bfloat16)

    for at, hub in enumerate(HUBS):
        ahead_ref[at] = block(-hub - 1)
    for at, source in enumerate(LOWER):
        behind_ref[at] = block(-HUBS[source] + 1)
    for at, hub in enumerate(HUBS):
        hub_ref[at] = block(hub)


def move(value, hops, nz):
    pairs = [(i, (i + (1 - 2 * (i // 2 % 2)) * 2 * hops) % nz) for i in range(nz)]
    return lax.ppermute(value, "z", pairs)


def shards(residual, norm_gain, gate_weight, up_weight, hidden_grad):
    nz, nh, nt = lax.axis_size("z"), lax.axis_size("yh"), lax.axis_size(TENSOR)
    rows, width = hidden_grad.shape
    features = residual.shape[1]
    depth = features // (nz * nh)
    f32, bf16 = jnp.float32, jnp.bfloat16
    flip = [(i, i ^ 1) for i in range(nz)]
    swap = [(0, 1), (1, 0)]
    near = jnp.concatenate([residual, lax.ppermute(residual, "z", flip)], axis=0)
    own = jnp.stack([hidden_grad, lax.ppermute(hidden_grad, "z", flip)])
    other = lax.ppermute(own, "yh", swap)
    chips = nh * nt // lax.axis_size("core")
    copies = jnp.broadcast_to(near[None], (chips,) + near.shape)
    same = lax.all_to_all(copies, ("yh", "x", "yl"), 0, 0, tiled=True)
    same = same.reshape(chips * near.shape[0], features)
    same, other = lax.optimization_barrier((same, other))
    swapped = lax.ppermute(same, "core", swap)
    factor = float(rows * nz * nh) ** (-0.5)
    shape = jax.ShapeDtypeStruct
    ahead, behind, hub, grads_own = pl.pallas_call(
        functools.partial(local_kernel, factor, nz, residual.shape[0]),
        out_shape=(
            shape((len(HUBS), depth, 2 * width), bf16),
            shape((len(LOWER), depth, 2 * width), bf16),
            shape((len(HUBS), depth, 2 * width), bf16),
            shape((rows, 2 * width), bf16),
        ),
        scratch_shapes=[
            pltpu.VMEM((2 * nh * rows, features), bf16),
            pltpu.VMEM((2 * nh * rows, 2 * width), bf16),
        ],
        compiler_params=pltpu.CompilerParams(vmem_limit_bytes=36 * 1024 * 1024),
        cost_estimate=pl.CostEstimate(
            flops=8 * nh * rows * features * width,
            bytes_accessed=8 * features * width,
            transcendentals=nh * rows * width,
        ),
        name="local",
    )(same, swapped, norm_gain.reshape(1, features), gate_weight.T, up_weight.T, own, other)

    ahead, behind = move(ahead, 1, nz), move(behind, -1, nz)
    grads_own, kept = lax.optimization_barrier((grads_own, hub))

    part = contract_last(grads_own[:, :width], gate_weight)
    part = (part + contract_last(grads_own[:, width:], up_weight)).astype(bf16)
    blocks = part.reshape(nt, rows // nt, features)
    moved = lax.all_to_all(blocks, TENSOR, 0, 0, tiled=True)

    plus, minus = lax.optimization_barrier(
        (
            (kept[1].astype(f32) + ahead[1].astype(f32)).astype(bf16),
            (kept[0].astype(f32) + ahead[0].astype(f32) + behind[0].astype(f32)).astype(bf16),
        )
    )
    plus, minus = move(plus, 3, nz), move(minus, -3, nz)
    total = kept[2].astype(f32) + ahead[2].astype(f32) + behind[1].astype(f32)
    total = (total + plus.astype(f32) + minus.astype(f32)).astype(bf16)

    scaled, inverse = normalize(residual)
    normed_grad = jnp.sum(moved.astype(f32), axis=0)
    weighted = normed_grad * norm_gain
    residual_grad = (
        (weighted - scaled * jnp.mean(weighted * scaled, axis=-1, keepdims=True)) * inverse
    ).astype(bf16)
    return (residual_grad, total[:, :width], total[:, width:])


def solution(mesh):
    fine = Mesh(mesh.devices.reshape(16, 2, 4, 2, 2), DP + TENSOR)
    return jax.shard_map(
        shards,
        mesh=fine,
        in_specs=(
            P(DP + TENSOR, None),
            P(),
            P(None, TENSOR),
            P(None, TENSOR),
            P(DP, TENSOR),
        ),
        out_specs=(P(DP + TENSOR, None), P(DP, TENSOR), P(DP, TENSOR)),
        check_vma=False,
    )
```

```python
import functools

import jax
import jax.numpy as jnp
from jax import lax
from jax.experimental import pallas as pl
from jax.experimental.pallas import tpu as pltpu
from jax.sharding import Mesh
from jax.sharding import PartitionSpec as P

EPSILON = 1e-05
DP = ("z", "yh")
TENSOR = ("x", "yl", "core")
OUTER = (-6, 6)
INNER = (-3, 0, 3)


def normalize(residual):
    values = residual.astype(jnp.float32)
    inverse = lax.rsqrt(jnp.mean(values * values, axis=-1, keepdims=True) + EPSILON)
    return (values * inverse, inverse)


def contract_last(left, right):
    return lax.dot_general(
        left, right, (((1,), (1,)), ((), ())), preferred_element_type=jnp.float32
    )


def contract_first(left, right):
    return lax.dot_general(
        left, right, (((0,), (0,)), ((), ())), preferred_element_type=jnp.float32
    )


def local_kernel(
    factor,
    nz,
    block_rows,
    same_ref,
    swapped_ref,
    gain_ref,
    gate_ref,
    up_ref,
    own_ref,
    other_ref,
    far_ref,
    outer_ahead_ref,
    outer_behind_ref,
    inner_ahead_ref,
    inner_behind_ref,
    outer_hub_ref,
    inner_hub_ref,
    grads_own_ref,
    normed_ref,
    grads_ref,
):
    z = lax.axis_index("z")
    half = lax.axis_index("yh")
    rows, width = own_ref.shape
    tokens = same_ref.shape[0]
    normed_ref[:tokens] = same_ref[...]
    normed_ref[tokens:] = (normalize(swapped_ref[...])[0] * gain_ref[...]).astype(jnp.bfloat16)
    normed = normed_ref[...]
    gate_value = contract_last(normed, gate_ref[...])
    up_value = contract_last(normed, up_ref[...])
    first = half == 0
    even = lax.axis_index("core") == 0
    count = lax.axis_size("core")
    split = (rows // (count * block_rows), count, block_rows, width)
    own = own_ref[...].astype(jnp.float32).reshape(split)
    other = other_ref[...].astype(jnp.float32).reshape(split)

    def by_core(values, same):
        near, away = (0, 1) if same else (1, 0)
        return jnp.where(even, values[:, near], values[:, away]).reshape(rows // count, width)

    pieces = []
    for same in (True, False):
        mine, theirs = by_core(own, same), by_core(other, same)
        pieces += [jnp.where(first, mine, theirs), jnp.where(first, theirs, mine)]
    upstream = jnp.concatenate(pieces, axis=0)
    sigmoid_gate = jax.nn.sigmoid(gate_value)
    weighted = upstream * sigmoid_gate
    gate_grad = weighted * up_value * (1.0 + gate_value * (1.0 - sigmoid_gate))
    up_grad = weighted * gate_value
    grads_ref[:, :width] = gate_grad.astype(jnp.bfloat16)
    grads_ref[:, width:] = up_grad.astype(jnp.bfloat16)
    piece = rows // count

    def own_rows(values):
        near = jnp.where(first, values[:piece], values[piece : 2 * piece])
        away = jnp.where(first, values[2 * piece : 3 * piece], values[3 * piece :])
        near = near.reshape(piece // block_rows, 1, block_rows, width)
        away = away.reshape(piece // block_rows, 1, block_rows, width)
        both = jnp.concatenate(
            [jnp.where(even, near, away), jnp.where(even, away, near)], axis=1
        )
        return both.reshape(rows, width).astype(jnp.bfloat16)

    grads_own_ref[:, :width] = own_rows(gate_grad)
    grads_own_ref[:, width:] = own_rows(up_grad)
    grads = grads_ref[...]
    depth = far_ref.shape[0]

    sign = 1 - 2 * lax.rem(z, 2)

    def block(relative):
        chunk = lax.rem(z - sign * relative + 2 * nz, nz)
        lanes = pl.ds(pl.multiple_of(chunk * 2 * depth, 2 * depth), 2 * depth)
        both = contract_first(normed_ref[:, lanes], grads) * factor
        return jnp.where(first, both[:depth], both[depth:]).astype(jnp.bfloat16)

    far_ref[...] = block(nz // 2)
    for at, hub in enumerate(OUTER):
        outer_ahead_ref[at] = block(-hub - 1)
        outer_behind_ref[at] = block(-hub + 1)
    for at, hub in enumerate(INNER):
        inner_ahead_ref[at] = block(-hub - 1)
        inner_behind_ref[at] = block(-hub + 1)
    for at, hub in enumerate(OUTER):
        outer_hub_ref[at] = block(hub)
    for at, hub in enumerate(INNER):
        inner_hub_ref[at] = block(hub)


def norm_kernel(rows_ref, gain_ref, normed_ref):
    normed_ref[...] = (normalize(rows_ref[...])[0] * gain_ref[...]).astype(jnp.bfloat16)


def move(value, hops, nz):
    pairs = [(i, (i + (1 - 2 * (i % 2)) * hops) % nz) for i in range(nz)]
    return lax.ppermute(value, "z", pairs)


def shards(residual, norm_gain, gate_weight, up_weight, hidden_grad):
    nz, nh, nt = lax.axis_size("z"), lax.axis_size("yh"), lax.axis_size(TENSOR)
    rows, width = hidden_grad.shape
    features = residual.shape[1]
    depth = features // (nz * nh)
    f32, bf16 = jnp.float32, jnp.bfloat16
    own = hidden_grad
    other = lax.ppermute(own, "yh", [(0, 1), (1, 0)])
    chips = nh * nt // lax.axis_size("core")
    copies = jnp.broadcast_to(residual[None], (chips,) + residual.shape)
    same = lax.all_to_all(copies, ("yh", "x", "yl"), 0, 0, tiled=True)
    same = same.reshape(chips * residual.shape[0], features)
    same, other = lax.optimization_barrier((same, other))
    swapped = lax.ppermute(same, "core", [(0, 1), (1, 0)])
    gain = norm_gain.reshape(1, features)
    normed_same = pl.pallas_call(
        norm_kernel,
        out_shape=jax.ShapeDtypeStruct(same.shape, bf16),
        cost_estimate=pl.CostEstimate(
            flops=8 * rows * features, bytes_accessed=4 * rows * features, transcendentals=rows
        ),
        compiler_params=pltpu.CompilerParams(vmem_limit_bytes=8 * 1024 * 1024),
        name="norm",
    )(same, gain)
    factor = float(rows * nz * nh) ** (-0.5)
    shape = jax.ShapeDtypeStruct
    far, outer_ahead, outer_behind, inner_ahead, inner_behind, outer_hub, inner_hub, grads_own = pl.pallas_call(
        functools.partial(local_kernel, factor, nz, residual.shape[0]),
        out_shape=(
            shape((depth, 2 * width), bf16),
            shape((len(OUTER), depth, 2 * width), bf16),
            shape((len(OUTER), depth, 2 * width), bf16),
            shape((len(INNER), depth, 2 * width), bf16),
            shape((len(INNER), depth, 2 * width), bf16),
            shape((len(OUTER), depth, 2 * width), bf16),
            shape((len(INNER), depth, 2 * width), bf16),
            shape((rows, 2 * width), bf16),
        ),
        scratch_shapes=[
            pltpu.VMEM((nh * rows, features), bf16),
            pltpu.VMEM((nh * rows, 2 * width), bf16),
        ],
        compiler_params=pltpu.CompilerParams(vmem_limit_bytes=20 * 1024 * 1024),
        cost_estimate=pl.CostEstimate(
            flops=8 * nh * rows * features * width,
            bytes_accessed=8 * features * width,
            transcendentals=nh * rows * width,
        ),
        name="local",
    )(normed_same, swapped, gain, gate_weight.T, up_weight.T, own, other)

    from_far = move(far, -2, nz).astype(f32)
    outer_ahead, outer_behind = move(outer_ahead, 1, nz), move(outer_behind, -1, nz)
    inner_ahead, inner_behind = move(inner_ahead, 1, nz), move(inner_behind, -1, nz)

    def outer(at):
        return (
            outer_hub[at].astype(f32)
            + outer_ahead[at].astype(f32)
            + outer_behind[at].astype(f32)
        )

    def inner(at, columns=slice(None)):
        return (
            inner_hub[at, :, columns].astype(f32)
            + inner_ahead[at, :, columns].astype(f32)
            + inner_behind[at, :, columns].astype(f32)
        )

    plus, minus = lax.optimization_barrier(
        (outer(0).astype(bf16), (outer(1) + from_far).astype(bf16))
    )
    grads_own, first_sum = lax.optimization_barrier((grads_own, plus))
    plus, minus = move(first_sum, 3, nz), move(minus, -3, nz)

    part = contract_last(grads_own[:, :width], gate_weight)
    part = (part + contract_last(grads_own[:, width:], up_weight)).astype(bf16)
    blocks = part.reshape(nt, rows // nt, features)
    moved = lax.all_to_all(blocks, TENSOR, 0, 0, tiled=True)

    plus, minus = lax.optimization_barrier((plus, minus))
    plus, minus = lax.optimization_barrier(
        (
            (inner(0) + minus.astype(f32)).astype(bf16),
            (inner(2) + plus.astype(f32)).astype(bf16),
        )
    )
    plus, minus = move(plus, 3, nz), move(minus, -3, nz)

    scaled, inverse = normalize(residual)
    normed_grad = jnp.sum(moved.astype(f32), axis=0)
    weighted = normed_grad * norm_gain
    residual_grad = (
        (weighted - scaled * jnp.mean(weighted * scaled, axis=-1, keepdims=True)) * inverse
    ).astype(bf16)
    totals = [
        (
            inner(1, columns)
            + plus[:, columns].astype(f32)
            + minus[:, columns].astype(f32)
        ).astype(bf16)
        for columns in (slice(0, width), slice(width, None))
    ]
    return (residual_grad, totals[0], totals[1])


def solution(mesh):
    fine = Mesh(mesh.devices.reshape(16, 2, 4, 2, 2), DP + TENSOR)
    return jax.shard_map(
        shards,
        mesh=fine,
        in_specs=(
            P(DP + TENSOR, None),
            P(),
            P(None, TENSOR),
            P(None, TENSOR),
            P(DP, TENSOR),
        ),
        out_specs=(P(DP + TENSOR, None), P(DP, TENSOR), P(DP, TENSOR)),
        check_vma=False,
    )
```

```python
import functools

import jax
import jax.numpy as jnp
from jax import lax
from jax.experimental import pallas as pl
from jax.experimental.pallas import tpu as pltpu
from jax.sharding import Mesh
from jax.sharding import PartitionSpec as P

EPSILON = 1e-05
DP = ("z", "yh")
TENSOR = ("x", "yl", "core")
OUTER = (-6, 6)
INNER = (-3, 0, 3)


def normalize(residual):
    values = residual.astype(jnp.float32)
    inverse = lax.rsqrt(jnp.mean(values * values, axis=-1, keepdims=True) + EPSILON)
    return (values * inverse, inverse)


def contract_last(left, right):
    return lax.dot_general(
        left, right, (((1,), (1,)), ((), ())), preferred_element_type=jnp.float32
    )


def contract_first(left, right):
    return lax.dot_general(
        left, right, (((0,), (0,)), ((), ())), preferred_element_type=jnp.float32
    )


def blocks_of(factor, nz, depth, normed_ref, grads_ref):
    z = lax.axis_index("z")
    first = lax.axis_index("yh") == 0
    sign = 1 - 2 * lax.rem(z, 2)
    grads = grads_ref[...]

    def block(relative):
        chunk = lax.rem(z - sign * relative + 2 * nz, nz)
        lanes = pl.ds(pl.multiple_of(chunk * 2 * depth, 2 * depth), 2 * depth)
        both = contract_first(normed_ref[:, lanes], grads) * factor
        return jnp.where(first, both[:depth], both[depth:]).astype(jnp.bfloat16)

    return block


def local_kernel(
    factor,
    nz,
    block_rows,
    same_ref,
    swapped_ref,
    gain_ref,
    gate_ref,
    up_ref,
    own_ref,
    other_ref,
    far_ref,
    outer_ahead_ref,
    outer_behind_ref,
    grads_own_ref,
    normed_ref,
    grads_ref,
):
    half = lax.axis_index("yh")
    rows, width = own_ref.shape
    tokens = same_ref.shape[0]
    normed_ref[:tokens] = same_ref[...]
    normed_ref[tokens:] = (normalize(swapped_ref[...])[0] * gain_ref[...]).astype(jnp.bfloat16)
    normed = normed_ref[...]
    gate_value = contract_last(normed, gate_ref[...])
    up_value = contract_last(normed, up_ref[...])
    first = half == 0
    even = lax.axis_index("core") == 0
    count = lax.axis_size("core")
    split = (rows // (count * block_rows), count, block_rows, width)
    own = own_ref[...].astype(jnp.float32).reshape(split)
    other = other_ref[...].astype(jnp.float32).reshape(split)

    def by_core(values, same):
        near, away = (0, 1) if same else (1, 0)
        return jnp.where(even, values[:, near], values[:, away]).reshape(rows // count, width)

    pieces = []
    for same in (True, False):
        mine, theirs = by_core(own, same), by_core(other, same)
        pieces += [jnp.where(first, mine, theirs), jnp.where(first, theirs, mine)]
    upstream = jnp.concatenate(pieces, axis=0)
    sigmoid_gate = jax.nn.sigmoid(gate_value)
    weighted = upstream * sigmoid_gate
    gate_grad = weighted * up_value * (1.0 + gate_value * (1.0 - sigmoid_gate))
    up_grad = weighted * gate_value
    grads_ref[:, :width] = gate_grad.astype(jnp.bfloat16)
    grads_ref[:, width:] = up_grad.astype(jnp.bfloat16)
    piece = rows // count

    def own_rows(values):
        near = jnp.where(first, values[:piece], values[piece : 2 * piece])
        away = jnp.where(first, values[2 * piece : 3 * piece], values[3 * piece :])
        near = near.reshape(piece // block_rows, 1, block_rows, width)
        away = away.reshape(piece // block_rows, 1, block_rows, width)
        both = jnp.concatenate(
            [jnp.where(even, near, away), jnp.where(even, away, near)], axis=1
        )
        return both.reshape(rows, width).astype(jnp.bfloat16)

    grads_own_ref[:, :width] = own_rows(gate_grad)
    grads_own_ref[:, width:] = own_rows(up_grad)
    block = blocks_of(factor, nz, far_ref.shape[0], normed_ref, grads_ref)
    far_ref[...] = block(nz // 2)
    for at, hub in enumerate(OUTER):
        outer_ahead_ref[at] = block(-hub - 1)
        outer_behind_ref[at] = block(-hub + 1)


def rest_kernel(
    factor,
    nz,
    normed_ref,
    grads_ref,
    inner_ahead_ref,
    inner_behind_ref,
    outer_hub_ref,
    inner_hub_ref,
):
    block = blocks_of(factor, nz, outer_hub_ref.shape[1], normed_ref, grads_ref)
    for at, hub in enumerate(INNER):
        inner_ahead_ref[at] = block(-hub - 1)
        inner_behind_ref[at] = block(-hub + 1)
    for at, hub in enumerate(OUTER):
        outer_hub_ref[at] = block(hub)
    for at, hub in enumerate(INNER):
        inner_hub_ref[at] = block(hub)


def f32_sum(*values):
    total = values[0].astype(jnp.float32)
    for value in values[1:]:
        total = total + value.astype(jnp.float32)
    return total


def outer_kernel(hub_ref, ahead_ref, behind_ref, far_ref, plus_ref, minus_ref):
    plus_ref[...] = f32_sum(hub_ref[0], ahead_ref[0], behind_ref[0]).astype(jnp.bfloat16)
    minus_ref[...] = f32_sum(hub_ref[1], ahead_ref[1], behind_ref[1], far_ref[...]).astype(
        jnp.bfloat16
    )


def inner_kernel(hub_ref, ahead_ref, behind_ref, upper_ref, lower_ref, plus_ref, minus_ref):
    plus_ref[...] = f32_sum(hub_ref[0], ahead_ref[0], behind_ref[0], lower_ref[...]).astype(
        jnp.bfloat16
    )
    minus_ref[...] = f32_sum(hub_ref[2], ahead_ref[2], behind_ref[2], upper_ref[...]).astype(
        jnp.bfloat16
    )


def total_kernel(hub_ref, ahead_ref, behind_ref, plus_ref, minus_ref, gate_ref, up_ref):
    width = gate_ref.shape[1]
    total = f32_sum(hub_ref[1], ahead_ref[1], behind_ref[1], plus_ref[...], minus_ref[...])
    gate_ref[...] = total[:, :width].astype(jnp.bfloat16)
    up_ref[...] = total[:, width:].astype(jnp.bfloat16)


def tail_kernel(rows_ref, gain_ref, moved_ref, out_ref):
    scaled, inverse = normalize(rows_ref[...])
    weighted = jnp.sum(moved_ref[...].astype(jnp.float32), axis=0) * gain_ref[...]
    mean = jnp.mean(weighted * scaled, axis=-1, keepdims=True)
    out_ref[...] = ((weighted - scaled * mean) * inverse).astype(jnp.bfloat16)


def call(kernel, name, shapes, *values):
    size = sum(value.size * 2 for value in values)
    return pl.pallas_call(
        kernel,
        out_shape=[jax.ShapeDtypeStruct(shape, jnp.bfloat16) for shape in shapes],
        compiler_params=pltpu.CompilerParams(vmem_limit_bytes=8 * 1024 * 1024),
        cost_estimate=pl.CostEstimate(flops=size, bytes_accessed=size, transcendentals=0),
        name=name,
    )(*values)


def norm_kernel(rows_ref, gain_ref, normed_ref):
    normed_ref[...] = (normalize(rows_ref[...])[0] * gain_ref[...]).astype(jnp.bfloat16)


def move(value, hops, nz):
    pairs = [(i, (i + (1 - 2 * (i % 2)) * hops) % nz) for i in range(nz)]
    return lax.ppermute(value, "z", pairs)


def shards(residual, norm_gain, gate_weight, up_weight, hidden_grad):
    nz, nh, nt = lax.axis_size("z"), lax.axis_size("yh"), lax.axis_size(TENSOR)
    rows, width = hidden_grad.shape
    features = residual.shape[1]
    depth = features // (nz * nh)
    f32, bf16 = jnp.float32, jnp.bfloat16
    own = hidden_grad
    other = lax.ppermute(own, "yh", [(0, 1), (1, 0)])
    chips = nh * nt // lax.axis_size("core")
    copies = jnp.broadcast_to(residual[None], (chips,) + residual.shape)
    same = lax.all_to_all(copies, ("yh", "x", "yl"), 0, 0, tiled=True)
    same = same.reshape(chips * residual.shape[0], features)
    same, other = lax.optimization_barrier((same, other))
    swapped = lax.ppermute(same, "core", [(0, 1), (1, 0)])
    gain = norm_gain.reshape(1, features)
    normed_same = pl.pallas_call(
        norm_kernel,
        out_shape=jax.ShapeDtypeStruct(same.shape, bf16),
        cost_estimate=pl.CostEstimate(
            flops=8 * rows * features, bytes_accessed=4 * rows * features, transcendentals=rows
        ),
        compiler_params=pltpu.CompilerParams(vmem_limit_bytes=8 * 1024 * 1024),
        name="norm",
    )(same, gain)
    factor = float(rows * nz * nh) ** (-0.5)
    shape = jax.ShapeDtypeStruct
    wide = 2 * width
    far, outer_ahead, outer_behind, grads_own, normed, grads = pl.pallas_call(
        functools.partial(local_kernel, factor, nz, residual.shape[0]),
        out_shape=[
            jax.ShapeDtypeStruct(shape, bf16)
            for shape in (
                (depth, wide),
                (len(OUTER), depth, wide),
                (len(OUTER), depth, wide),
                (rows, wide),
                (nh * rows, features),
                (nh * rows, wide),
            )
        ],
        compiler_params=pltpu.CompilerParams(vmem_limit_bytes=20 * 1024 * 1024),
        cost_estimate=pl.CostEstimate(
            flops=6 * nh * rows * features * width,
            bytes_accessed=8 * features * width,
            transcendentals=nh * rows * width,
        ),
        name="local",
    )(normed_same, swapped, gain, gate_weight.T, up_weight.T, own, other)
    inner_ahead, inner_behind, outer_hub, inner_hub = pl.pallas_call(
        functools.partial(rest_kernel, factor, nz),
        out_shape=[
            jax.ShapeDtypeStruct((count, depth, wide), bf16)
            for count in (len(INNER), len(INNER), len(OUTER), len(INNER))
        ],
        compiler_params=pltpu.CompilerParams(vmem_limit_bytes=12 * 1024 * 1024),
        cost_estimate=pl.CostEstimate(
            flops=4 * nh * rows * features * width,
            bytes_accessed=4 * nh * rows * features,
            transcendentals=0,
        ),
        name="rest",
    )(normed, grads)

    from_far = move(far, -2, nz).astype(f32)
    outer_ahead, outer_behind = move(outer_ahead, 1, nz), move(outer_behind, -1, nz)
    inner_ahead, inner_behind = move(inner_ahead, 1, nz), move(inner_behind, -1, nz)

    def outer(at):
        return (
            outer_hub[at].astype(f32)
            + outer_ahead[at].astype(f32)
            + outer_behind[at].astype(f32)
        )

    def inner(at, columns=slice(None)):
        return (
            inner_hub[at, :, columns].astype(f32)
            + inner_ahead[at, :, columns].astype(f32)
            + inner_behind[at, :, columns].astype(f32)
        )

    plus, minus = lax.optimization_barrier(
        (outer(0).astype(bf16), (outer(1) + from_far).astype(bf16))
    )
    grads_own, first_sum = lax.optimization_barrier((grads_own, plus))
    plus, minus = move(first_sum, 3, nz), move(minus, -3, nz)

    part = contract_last(grads_own[:, :width], gate_weight)
    part = (part + contract_last(grads_own[:, width:], up_weight)).astype(bf16)
    blocks = part.reshape(nt, rows // nt, features)
    moved = lax.all_to_all(blocks, TENSOR, 0, 0, tiled=True)

    plus, minus = lax.optimization_barrier((plus, minus))
    plus, minus = lax.optimization_barrier(
        (
            (inner(0) + minus.astype(f32)).astype(bf16),
            (inner(2) + plus.astype(f32)).astype(bf16),
        )
    )
    plus, minus = move(plus, 3, nz), move(minus, -3, nz)

    scaled, inverse = normalize(residual)
    normed_grad = jnp.sum(moved.astype(f32), axis=0)
    weighted = normed_grad * norm_gain
    residual_grad = (
        (weighted - scaled * jnp.mean(weighted * scaled, axis=-1, keepdims=True)) * inverse
    ).astype(bf16)
    totals = call(
        total_kernel,
        "total",
        [(depth, width)] * 2,
        inner_hub,
        inner_ahead,
        inner_behind,
        plus,
        minus,
    )
    return (residual_grad, totals[0], totals[1])


def solution(mesh):
    fine = Mesh(mesh.devices.reshape(16, 2, 4, 2, 2), DP + TENSOR)
    return jax.shard_map(
        shards,
        mesh=fine,
        in_specs=(
            P(DP + TENSOR, None),
            P(),
            P(None, TENSOR),
            P(None, TENSOR),
            P(DP, TENSOR),
        ),
        out_specs=(P(DP + TENSOR, None), P(DP, TENSOR), P(DP, TENSOR)),
        check_vma=False,
    )
```

```python
import functools

import jax
import jax.numpy as jnp
from jax import lax
from jax.experimental import pallas as pl
from jax.experimental.pallas import tpu as pltpu
from jax.sharding import Mesh
from jax.sharding import PartitionSpec as P

EPSILON = 1e-05
DP = ("z", "yh")
TENSOR = ("x", "yl", "core")
OUTER = (-6, 6)
INNER = (-3, 0, 3)


def normalize(residual):
    values = residual.astype(jnp.float32)
    inverse = lax.rsqrt(jnp.mean(values * values, axis=-1, keepdims=True) + EPSILON)
    return (values * inverse, inverse)


def contract_last(left, right):
    return lax.dot_general(
        left, right, (((1,), (1,)), ((), ())), preferred_element_type=jnp.float32
    )


def contract_first(left, right):
    return lax.dot_general(
        left, right, (((0,), (0,)), ((), ())), preferred_element_type=jnp.float32
    )


def blocks_of(factor, nz, depth, normed_ref, grads_ref):
    z = lax.axis_index("z")
    first = lax.axis_index("yh") == 0
    sign = 1 - 2 * lax.rem(z, 2)
    grads = grads_ref[...]

    def block(relative):
        chunk = lax.rem(z - sign * relative + 2 * nz, nz)
        lanes = pl.ds(pl.multiple_of(chunk * 2 * depth, 2 * depth), 2 * depth)
        both = contract_first(normed_ref[:, lanes], grads) * factor
        return jnp.where(first, both[:depth], both[depth:]).astype(jnp.bfloat16)

    return block


def local_kernel(
    factor,
    nz,
    block_rows,
    same_ref,
    swapped_ref,
    gain_ref,
    gate_ref,
    up_ref,
    own_ref,
    other_ref,
    far_ref,
    outer_ahead_ref,
    outer_behind_ref,
    grads_own_ref,
    normed_ref,
    grads_ref,
):
    half = lax.axis_index("yh")
    rows, width = own_ref.shape
    tokens = same_ref.shape[0]
    normed_ref[:tokens] = same_ref[...]
    normed_ref[tokens:] = (normalize(swapped_ref[...])[0] * gain_ref[...]).astype(jnp.bfloat16)
    normed = normed_ref[...]
    gate_value = contract_last(normed, gate_ref[...])
    up_value = contract_last(normed, up_ref[...])
    first = half == 0
    even = lax.axis_index("core") == 0
    count = lax.axis_size("core")
    split = (rows // (count * block_rows), count, block_rows, width)
    own = own_ref[...].astype(jnp.float32).reshape(split)
    other = other_ref[...].astype(jnp.float32).reshape(split)

    def by_core(values, same):
        near, away = (0, 1) if same else (1, 0)
        return jnp.where(even, values[:, near], values[:, away]).reshape(rows // count, width)

    pieces = []
    for same in (True, False):
        mine, theirs = by_core(own, same), by_core(other, same)
        pieces += [jnp.where(first, mine, theirs), jnp.where(first, theirs, mine)]
    upstream = jnp.concatenate(pieces, axis=0)
    sigmoid_gate = jax.nn.sigmoid(gate_value)
    weighted = upstream * sigmoid_gate
    gate_grad = weighted * up_value * (1.0 + gate_value * (1.0 - sigmoid_gate))
    up_grad = weighted * gate_value
    grads_ref[:, :width] = gate_grad.astype(jnp.bfloat16)
    grads_ref[:, width:] = up_grad.astype(jnp.bfloat16)
    piece = rows // count

    def own_rows(values):
        near = jnp.where(first, values[:piece], values[piece : 2 * piece])
        away = jnp.where(first, values[2 * piece : 3 * piece], values[3 * piece :])
        near = near.reshape(piece // block_rows, 1, block_rows, width)
        away = away.reshape(piece // block_rows, 1, block_rows, width)
        both = jnp.concatenate(
            [jnp.where(even, near, away), jnp.where(even, away, near)], axis=1
        )
        return both.reshape(rows, width).astype(jnp.bfloat16)

    grads_own_ref[:, :width] = own_rows(gate_grad)
    grads_own_ref[:, width:] = own_rows(up_grad)
    block = blocks_of(factor, nz, far_ref.shape[0], normed_ref, grads_ref)
    far_ref[...] = block(nz // 2)
    for at, hub in enumerate(OUTER):
        outer_ahead_ref[at] = block(-hub - 1)
        outer_behind_ref[at] = block(-hub + 1)


def rest_kernel(
    factor,
    nz,
    normed_ref,
    grads_ref,
    grads_own_ref,
    gate_ref,
    up_ref,
    inner_ahead_ref,
    inner_behind_ref,
    outer_hub_ref,
    inner_hub_ref,
    part_ref,
):
    width = gate_ref.shape[0]
    block = blocks_of(factor, nz, outer_hub_ref.shape[1], normed_ref, grads_ref)
    for at, hub in enumerate(INNER):
        inner_ahead_ref[at] = block(-hub - 1)
        inner_behind_ref[at] = block(-hub + 1)
    for at, hub in enumerate(OUTER):
        outer_hub_ref[at] = block(hub)
    for at, hub in enumerate(INNER):
        inner_hub_ref[at] = block(hub)
    f32 = jnp.float32
    gate_part = jnp.dot(grads_own_ref[:, :width], gate_ref[...], preferred_element_type=f32)
    up_part = jnp.dot(grads_own_ref[:, width:], up_ref[...], preferred_element_type=f32)
    part_ref[...] = (gate_part + up_part).astype(jnp.bfloat16)


def f32_sum(*values):
    total = values[0].astype(jnp.float32)
    for value in values[1:]:
        total = total + value.astype(jnp.float32)
    return total


def outer_kernel(hub_ref, ahead_ref, behind_ref, far_ref, plus_ref, minus_ref):
    plus_ref[...] = f32_sum(hub_ref[0], ahead_ref[0], behind_ref[0]).astype(jnp.bfloat16)
    minus_ref[...] = f32_sum(hub_ref[1], ahead_ref[1], behind_ref[1], far_ref[...]).astype(
        jnp.bfloat16
    )


def inner_kernel(hub_ref, ahead_ref, behind_ref, upper_ref, lower_ref, plus_ref, minus_ref):
    plus_ref[...] = f32_sum(hub_ref[0], ahead_ref[0], behind_ref[0], lower_ref[...]).astype(
        jnp.bfloat16
    )
    minus_ref[...] = f32_sum(hub_ref[2], ahead_ref[2], behind_ref[2], upper_ref[...]).astype(
        jnp.bfloat16
    )


def total_kernel(hub_ref, ahead_ref, behind_ref, plus_ref, minus_ref, gate_ref, up_ref):
    width = gate_ref.shape[1]
    total = f32_sum(hub_ref[1], ahead_ref[1], behind_ref[1], plus_ref[...], minus_ref[...])
    gate_ref[...] = total[:, :width].astype(jnp.bfloat16)
    up_ref[...] = total[:, width:].astype(jnp.bfloat16)


def tail_kernel(rows_ref, gain_ref, moved_ref, out_ref):
    scaled, inverse = normalize(rows_ref[...])
    weighted = jnp.sum(moved_ref[...].astype(jnp.float32), axis=0) * gain_ref[...]
    mean = jnp.mean(weighted * scaled, axis=-1, keepdims=True)
    out_ref[...] = ((weighted - scaled * mean) * inverse).astype(jnp.bfloat16)


def call(kernel, name, shapes, *values):
    size = sum(value.size * 2 for value in values)
    return pl.pallas_call(
        kernel,
        out_shape=[jax.ShapeDtypeStruct(shape, jnp.bfloat16) for shape in shapes],
        compiler_params=pltpu.CompilerParams(vmem_limit_bytes=8 * 1024 * 1024),
        cost_estimate=pl.CostEstimate(flops=size, bytes_accessed=size, transcendentals=0),
        name=name,
    )(*values)


def norm_kernel(rows_ref, gain_ref, normed_ref):
    normed_ref[...] = (normalize(rows_ref[...])[0] * gain_ref[...]).astype(jnp.bfloat16)


def move(value, hops, nz):
    pairs = [(i, (i + (1 - 2 * (i % 2)) * hops) % nz) for i in range(nz)]
    return lax.ppermute(value, "z", pairs)


def shards(residual, norm_gain, gate_weight, up_weight, hidden_grad):
    nz, nh, nt = lax.axis_size("z"), lax.axis_size("yh"), lax.axis_size(TENSOR)
    rows, width = hidden_grad.shape
    features = residual.shape[1]
    depth = features // (nz * nh)
    f32, bf16 = jnp.float32, jnp.bfloat16
    own = hidden_grad
    other = lax.ppermute(own, "yh", [(0, 1), (1, 0)])
    chips = nh * nt // lax.axis_size("core")
    copies = jnp.broadcast_to(residual[None], (chips,) + residual.shape)
    same = lax.all_to_all(copies, ("yh", "x", "yl"), 0, 0, tiled=True)
    same = same.reshape(chips * residual.shape[0], features)
    same, other = lax.optimization_barrier((same, other))
    swapped = lax.ppermute(same, "core", [(0, 1), (1, 0)])
    gain = norm_gain.reshape(1, features)
    normed_same = pl.pallas_call(
        norm_kernel,
        out_shape=jax.ShapeDtypeStruct(same.shape, bf16),
        cost_estimate=pl.CostEstimate(
            flops=8 * rows * features, bytes_accessed=4 * rows * features, transcendentals=rows
        ),
        compiler_params=pltpu.CompilerParams(vmem_limit_bytes=8 * 1024 * 1024),
        name="norm",
    )(same, gain)
    factor = float(rows * nz * nh) ** (-0.5)
    shape = jax.ShapeDtypeStruct
    wide = 2 * width
    far, outer_ahead, outer_behind, grads_own, normed, grads = pl.pallas_call(
        functools.partial(local_kernel, factor, nz, residual.shape[0]),
        out_shape=[
            jax.ShapeDtypeStruct(shape, bf16)
            for shape in (
                (depth, wide),
                (len(OUTER), depth, wide),
                (len(OUTER), depth, wide),
                (rows, wide),
                (nh * rows, features),
                (nh * rows, wide),
            )
        ],
        compiler_params=pltpu.CompilerParams(vmem_limit_bytes=20 * 1024 * 1024),
        cost_estimate=pl.CostEstimate(
            flops=6 * nh * rows * features * width,
            bytes_accessed=8 * features * width,
            transcendentals=nh * rows * width,
        ),
        name="local",
    )(normed_same, swapped, gain, gate_weight.T, up_weight.T, own, other)
    inner_ahead, inner_behind, outer_hub, inner_hub, part = pl.pallas_call(
        functools.partial(rest_kernel, factor, nz),
        out_shape=[
            jax.ShapeDtypeStruct((count, depth, wide), bf16)
            for count in (len(INNER), len(INNER), len(OUTER), len(INNER))
        ]
        + [jax.ShapeDtypeStruct((rows, features), bf16)],
        compiler_params=pltpu.CompilerParams(vmem_limit_bytes=16 * 1024 * 1024),
        cost_estimate=pl.CostEstimate(
            flops=6 * nh * rows * features * width,
            bytes_accessed=8 * nh * rows * features,
            transcendentals=0,
        ),
        name="rest",
    )(normed, grads, grads_own, gate_weight.T, up_weight.T)

    far_in = move(far, -2, nz)
    outer_ahead, outer_behind = move(outer_ahead, 1, nz), move(outer_behind, -1, nz)
    inner_ahead, inner_behind = move(inner_ahead, 1, nz), move(inner_behind, -1, nz)

    def outer(at):
        return (
            outer_hub[at].astype(f32)
            + outer_ahead[at].astype(f32)
            + outer_behind[at].astype(f32)
        )

    def inner(at, columns=slice(None)):
        return (
            inner_hub[at, :, columns].astype(f32)
            + inner_ahead[at, :, columns].astype(f32)
            + inner_behind[at, :, columns].astype(f32)
        )

    plus, minus = call(
        outer_kernel, "outer", [(depth, wide)] * 2, outer_hub, outer_ahead, outer_behind, far_in
    )
    part, first_sum = lax.optimization_barrier((part, plus))
    plus, minus = move(first_sum, 3, nz), move(minus, -3, nz)

    blocks = part.reshape(nt, rows // nt, features)
    moved = lax.all_to_all(blocks, TENSOR, 0, 0, tiled=True)

    plus, minus = lax.optimization_barrier((plus, minus))
    plus, minus = lax.optimization_barrier(
        (
            (inner(0) + minus.astype(f32)).astype(bf16),
            (inner(2) + plus.astype(f32)).astype(bf16),
        )
    )
    plus, minus = move(plus, 3, nz), move(minus, -3, nz)

    scaled, inverse = normalize(residual)
    normed_grad = jnp.sum(moved.astype(f32), axis=0)
    weighted = normed_grad * norm_gain
    residual_grad = (
        (weighted - scaled * jnp.mean(weighted * scaled, axis=-1, keepdims=True)) * inverse
    ).astype(bf16)
    totals = call(
        total_kernel,
        "total",
        [(depth, width)] * 2,
        inner_hub,
        inner_ahead,
        inner_behind,
        plus,
        minus,
    )
    return (residual_grad, totals[0], totals[1])


def solution(mesh):
    fine = Mesh(mesh.devices.reshape(16, 2, 4, 2, 2), DP + TENSOR)
    return jax.shard_map(
        shards,
        mesh=fine,
        in_specs=(
            P(DP + TENSOR, None),
            P(),
            P(None, TENSOR),
            P(None, TENSOR),
            P(DP, TENSOR),
        ),
        out_specs=(P(DP + TENSOR, None), P(DP, TENSOR), P(DP, TENSOR)),
        check_vma=False,
    )
```

```python
import functools

import jax
import jax.numpy as jnp
from jax import lax
from jax.experimental import pallas as pl
from jax.experimental.pallas import tpu as pltpu
from jax.sharding import Mesh
from jax.sharding import PartitionSpec as P

EPSILON = 1e-05
DP = ("z", "yh")
TENSOR = ("x", "yl", "core")
OUTER = (-6, 6)
INNER = (-3, 0, 3)


def normalize(residual):
    values = residual.astype(jnp.float32)
    inverse = lax.rsqrt(jnp.mean(values * values, axis=-1, keepdims=True) + EPSILON)
    return (values * inverse, inverse)


def contract_last(left, right):
    return lax.dot_general(
        left, right, (((1,), (1,)), ((), ())), preferred_element_type=jnp.float32
    )


def contract_first(left, right):
    return lax.dot_general(
        left, right, (((0,), (0,)), ((), ())), preferred_element_type=jnp.float32
    )


def blocks_of(factor, nz, depth, normed_ref, grads_ref):
    z = lax.axis_index("z")
    first = lax.axis_index("yh") == 0
    sign = 1 - 2 * lax.rem(z, 2)
    grads = grads_ref[...]

    def block(relative):
        chunk = lax.rem(z - sign * relative + 2 * nz, nz)
        lanes = pl.ds(pl.multiple_of(chunk * 2 * depth, 2 * depth), 2 * depth)
        both = contract_first(normed_ref[:, lanes], grads) * factor
        return jnp.where(first, both[:depth], both[depth:]).astype(jnp.bfloat16)

    return block


def local_kernel(
    factor,
    nz,
    block_rows,
    same_ref,
    up_same_ref,
    swapped_ref,
    gain_ref,
    gate_ref,
    up_ref,
    own_ref,
    other_ref,
    far_ref,
    outer_ahead_ref,
    outer_behind_ref,
    grads_own_ref,
    normed_ref,
    grads_ref,
):
    half = lax.axis_index("yh")
    rows, width = own_ref.shape
    tokens = same_ref.shape[0]
    normed_ref[:tokens] = same_ref[...]
    normed_ref[tokens:] = (normalize(swapped_ref[...])[0] * gain_ref[...]).astype(jnp.bfloat16)
    normed = normed_ref[...]
    gate_value = contract_last(normed, gate_ref[...])
    up_swapped = contract_last(normed_ref[tokens:], up_ref[...])
    up_value = jnp.concatenate([up_same_ref[...], up_swapped], axis=0)
    first = half == 0
    even = lax.axis_index("core") == 0
    count = lax.axis_size("core")
    split = (rows // (count * block_rows), count, block_rows, width)
    own = own_ref[...].astype(jnp.float32).reshape(split)
    other = other_ref[...].astype(jnp.float32).reshape(split)

    def by_core(values, same):
        near, away = (0, 1) if same else (1, 0)
        return jnp.where(even, values[:, near], values[:, away]).reshape(rows // count, width)

    pieces = []
    for same in (True, False):
        mine, theirs = by_core(own, same), by_core(other, same)
        pieces += [jnp.where(first, mine, theirs), jnp.where(first, theirs, mine)]
    upstream = jnp.concatenate(pieces, axis=0)
    sigmoid_gate = jax.nn.sigmoid(gate_value)
    weighted = upstream * sigmoid_gate
    gate_grad = weighted * up_value * (1.0 + gate_value * (1.0 - sigmoid_gate))
    up_grad = weighted * gate_value
    grads_ref[:, :width] = gate_grad.astype(jnp.bfloat16)
    grads_ref[:, width:] = up_grad.astype(jnp.bfloat16)
    piece = rows // count

    def own_rows(values):
        near = jnp.where(first, values[:piece], values[piece : 2 * piece])
        away = jnp.where(first, values[2 * piece : 3 * piece], values[3 * piece :])
        near = near.reshape(piece // block_rows, 1, block_rows, width)
        away = away.reshape(piece // block_rows, 1, block_rows, width)
        both = jnp.concatenate(
            [jnp.where(even, near, away), jnp.where(even, away, near)], axis=1
        )
        return both.reshape(rows, width).astype(jnp.bfloat16)

    grads_own_ref[:, :width] = own_rows(gate_grad)
    grads_own_ref[:, width:] = own_rows(up_grad)
    block = blocks_of(factor, nz, far_ref.shape[0], normed_ref, grads_ref)
    far_ref[...] = block(nz // 2)
    for at, hub in enumerate(OUTER):
        outer_ahead_ref[at] = block(-hub - 1)
        outer_behind_ref[at] = block(-hub + 1)


def rest_kernel(
    factor,
    nz,
    normed_ref,
    grads_ref,
    inner_ahead_ref,
    inner_behind_ref,
    outer_hub_ref,
    inner_hub_ref,
):
    block = blocks_of(factor, nz, outer_hub_ref.shape[1], normed_ref, grads_ref)
    for at, hub in enumerate(INNER):
        inner_ahead_ref[at] = block(-hub - 1)
        inner_behind_ref[at] = block(-hub + 1)
    for at, hub in enumerate(OUTER):
        outer_hub_ref[at] = block(hub)
    for at, hub in enumerate(INNER):
        inner_hub_ref[at] = block(hub)


def f32_sum(*values):
    total = values[0].astype(jnp.float32)
    for value in values[1:]:
        total = total + value.astype(jnp.float32)
    return total


def outer_kernel(hub_ref, ahead_ref, behind_ref, far_ref, plus_ref, minus_ref):
    plus_ref[...] = f32_sum(hub_ref[0], ahead_ref[0], behind_ref[0]).astype(jnp.bfloat16)
    minus_ref[...] = f32_sum(hub_ref[1], ahead_ref[1], behind_ref[1], far_ref[...]).astype(
        jnp.bfloat16
    )


def inner_kernel(hub_ref, ahead_ref, behind_ref, upper_ref, lower_ref, plus_ref, minus_ref):
    plus_ref[...] = f32_sum(hub_ref[0], ahead_ref[0], behind_ref[0], lower_ref[...]).astype(
        jnp.bfloat16
    )
    minus_ref[...] = f32_sum(hub_ref[2], ahead_ref[2], behind_ref[2], upper_ref[...]).astype(
        jnp.bfloat16
    )


def total_kernel(hub_ref, ahead_ref, behind_ref, plus_ref, minus_ref, gate_ref, up_ref):
    width = gate_ref.shape[1]
    total = f32_sum(hub_ref[1], ahead_ref[1], behind_ref[1], plus_ref[...], minus_ref[...])
    gate_ref[...] = total[:, :width].astype(jnp.bfloat16)
    up_ref[...] = total[:, width:].astype(jnp.bfloat16)


def tail_kernel(rows_ref, gain_ref, moved_ref, out_ref):
    scaled, inverse = normalize(rows_ref[...])
    weighted = jnp.sum(moved_ref[...].astype(jnp.float32), axis=0) * gain_ref[...]
    mean = jnp.mean(weighted * scaled, axis=-1, keepdims=True)
    out_ref[...] = ((weighted - scaled * mean) * inverse).astype(jnp.bfloat16)


def call(kernel, name, shapes, *values):
    size = sum(value.size * 2 for value in values)
    return pl.pallas_call(
        kernel,
        out_shape=[jax.ShapeDtypeStruct(shape, jnp.bfloat16) for shape in shapes],
        compiler_params=pltpu.CompilerParams(vmem_limit_bytes=8 * 1024 * 1024),
        cost_estimate=pl.CostEstimate(flops=size, bytes_accessed=size, transcendentals=0),
        name=name,
    )(*values)


def norm_kernel(rows_ref, gain_ref, up_ref, normed_ref, value_ref):
    normed_ref[...] = (normalize(rows_ref[...])[0] * gain_ref[...]).astype(jnp.bfloat16)
    value_ref[...] = contract_last(normed_ref[...], up_ref[...])


def move(value, hops, nz):
    pairs = [(i, (i + (1 - 2 * (i % 2)) * hops) % nz) for i in range(nz)]
    return lax.ppermute(value, "z", pairs)


def shards(residual, norm_gain, gate_weight, up_weight, hidden_grad):
    nz, nh, nt = lax.axis_size("z"), lax.axis_size("yh"), lax.axis_size(TENSOR)
    rows, width = hidden_grad.shape
    features = residual.shape[1]
    depth = features // (nz * nh)
    f32, bf16 = jnp.float32, jnp.bfloat16
    own = hidden_grad
    other = lax.ppermute(own, "yh", [(0, 1), (1, 0)])
    chips = nh * nt // lax.axis_size("core")
    copies = jnp.broadcast_to(residual[None], (chips,) + residual.shape)
    same = lax.all_to_all(copies, ("yh", "x", "yl"), 0, 0, tiled=True)
    same = same.reshape(chips * residual.shape[0], features)
    same, other = lax.optimization_barrier((same, other))
    swapped = lax.ppermute(same, "core", [(0, 1), (1, 0)])
    gain = norm_gain.reshape(1, features)
    normed_same, up_same = pl.pallas_call(
        norm_kernel,
        out_shape=[
            jax.ShapeDtypeStruct(same.shape, bf16),
            jax.ShapeDtypeStruct((same.shape[0], width), f32),
        ],
        cost_estimate=pl.CostEstimate(
            flops=8 * rows * features, bytes_accessed=4 * rows * features, transcendentals=rows
        ),
        compiler_params=pltpu.CompilerParams(vmem_limit_bytes=8 * 1024 * 1024),
        name="norm",
    )(same, gain, up_weight.T)
    factor = float(rows * nz * nh) ** (-0.5)
    shape = jax.ShapeDtypeStruct
    wide = 2 * width
    far, outer_ahead, outer_behind, grads_own, normed, grads = pl.pallas_call(
        functools.partial(local_kernel, factor, nz, residual.shape[0]),
        out_shape=[
            jax.ShapeDtypeStruct(shape, bf16)
            for shape in (
                (depth, wide),
                (len(OUTER), depth, wide),
                (len(OUTER), depth, wide),
                (rows, wide),
                (nh * rows, features),
                (nh * rows, wide),
            )
        ],
        compiler_params=pltpu.CompilerParams(vmem_limit_bytes=20 * 1024 * 1024),
        cost_estimate=pl.CostEstimate(
            flops=6 * nh * rows * features * width,
            bytes_accessed=8 * features * width,
            transcendentals=nh * rows * width,
        ),
        name="local",
    )(normed_same, up_same, swapped, gain, gate_weight.T, up_weight.T, own, other)
    inner_ahead, inner_behind, outer_hub, inner_hub = pl.pallas_call(
        functools.partial(rest_kernel, factor, nz),
        out_shape=[
            jax.ShapeDtypeStruct((count, depth, wide), bf16)
            for count in (len(INNER), len(INNER), len(OUTER), len(INNER))
        ],
        compiler_params=pltpu.CompilerParams(vmem_limit_bytes=12 * 1024 * 1024),
        cost_estimate=pl.CostEstimate(
            flops=4 * nh * rows * features * width,
            bytes_accessed=4 * nh * rows * features,
            transcendentals=0,
        ),
        name="rest",
    )(normed, grads)

    from_far = move(far, -2, nz).astype(f32)
    outer_ahead, outer_behind = move(outer_ahead, 1, nz), move(outer_behind, -1, nz)
    inner_ahead, inner_behind = move(inner_ahead, 1, nz), move(inner_behind, -1, nz)

    def outer(at):
        return (
            outer_hub[at].astype(f32)
            + outer_ahead[at].astype(f32)
            + outer_behind[at].astype(f32)
        )

    def inner(at, columns=slice(None)):
        return (
            inner_hub[at, :, columns].astype(f32)
            + inner_ahead[at, :, columns].astype(f32)
            + inner_behind[at, :, columns].astype(f32)
        )

    plus, minus = lax.optimization_barrier(
        (outer(0).astype(bf16), (outer(1) + from_far).astype(bf16))
    )
    grads_own, first_sum = lax.optimization_barrier((grads_own, plus))
    plus, minus = move(first_sum, 3, nz), move(minus, -3, nz)

    part = contract_last(grads_own[:, :width], gate_weight)
    part = (part + contract_last(grads_own[:, width:], up_weight)).astype(bf16)
    blocks = part.reshape(nt, rows // nt, features)
    moved = lax.all_to_all(blocks, TENSOR, 0, 0, tiled=True)

    plus, minus = lax.optimization_barrier((plus, minus))
    plus, minus = lax.optimization_barrier(
        (
            (inner(0) + minus.astype(f32)).astype(bf16),
            (inner(2) + plus.astype(f32)).astype(bf16),
        )
    )
    plus, minus = move(plus, 3, nz), move(minus, -3, nz)

    scaled, inverse = normalize(residual)
    normed_grad = jnp.sum(moved.astype(f32), axis=0)
    weighted = normed_grad * norm_gain
    residual_grad = (
        (weighted - scaled * jnp.mean(weighted * scaled, axis=-1, keepdims=True)) * inverse
    ).astype(bf16)
    totals = call(
        total_kernel,
        "total",
        [(depth, width)] * 2,
        inner_hub,
        inner_ahead,
        inner_behind,
        plus,
        minus,
    )
    return (residual_grad, totals[0], totals[1])


def solution(mesh):
    fine = Mesh(mesh.devices.reshape(16, 2, 4, 2, 2), DP + TENSOR)
    return jax.shard_map(
        shards,
        mesh=fine,
        in_specs=(
            P(DP + TENSOR, None),
            P(),
            P(None, TENSOR),
            P(None, TENSOR),
            P(DP, TENSOR),
        ),
        out_specs=(P(DP + TENSOR, None), P(DP, TENSOR), P(DP, TENSOR)),
        check_vma=False,
    )
```

```python
import functools

import jax
import jax.numpy as jnp
from jax import lax
from jax.experimental import pallas as pl
from jax.experimental.pallas import tpu as pltpu
from jax.sharding import Mesh
from jax.sharding import PartitionSpec as P

EPSILON = 1e-05
DP = ("z", "yh")
TENSOR = ("x", "yl", "core")
OUTER = (-6, 6)
INNER = (-3, 0, 3)


def normalize(residual):
    values = residual.astype(jnp.float32)
    inverse = lax.rsqrt(jnp.mean(values * values, axis=-1, keepdims=True) + EPSILON)
    return (values * inverse, inverse)


def contract_last(left, right):
    return lax.dot_general(
        left, right, (((1,), (1,)), ((), ())), preferred_element_type=jnp.float32
    )


def contract_first(left, right):
    return lax.dot_general(
        left, right, (((0,), (0,)), ((), ())), preferred_element_type=jnp.float32
    )


def blocks_of(factor, nz, depth, normed_ref, grads_ref):
    z = lax.axis_index("z")
    first = lax.axis_index("yh") == 0
    sign = 1 - 2 * lax.rem(z, 2)
    grads = grads_ref[...]

    def block(relative):
        chunk = lax.rem(z - sign * relative + 2 * nz, nz)
        lanes = pl.ds(pl.multiple_of(chunk * 2 * depth, 2 * depth), 2 * depth)
        both = contract_first(normed_ref[:, lanes], grads) * factor
        return jnp.where(first, both[:depth], both[depth:]).astype(jnp.bfloat16)

    return block


def local_kernel(
    factor,
    nz,
    block_rows,
    same_ref,
    up_same_ref,
    swapped_ref,
    gain_ref,
    gate_ref,
    up_ref,
    own_ref,
    other_ref,
    far_ref,
    outer_ahead_ref,
    outer_behind_ref,
    grads_own_ref,
    normed_ref,
    grads_ref,
):
    half = lax.axis_index("yh")
    rows, width = own_ref.shape
    tokens = same_ref.shape[0]
    normed_ref[:tokens] = same_ref[...]
    normed_ref[tokens:] = (normalize(swapped_ref[...])[0] * gain_ref[...]).astype(jnp.bfloat16)
    normed = normed_ref[...]
    gate_value = contract_last(normed, gate_ref[...])
    up_swapped = contract_last(normed_ref[tokens:], up_ref[...])
    up_value = jnp.concatenate([up_same_ref[...], up_swapped], axis=0)
    first = half == 0
    even = lax.axis_index("core") == 0
    count = lax.axis_size("core")
    split = (rows // (count * block_rows), count, block_rows, width)
    own = own_ref[...].astype(jnp.float32).reshape(split)
    other = other_ref[...].astype(jnp.float32).reshape(split)

    def by_core(values, same):
        near, away = (0, 1) if same else (1, 0)
        return jnp.where(even, values[:, near], values[:, away]).reshape(rows // count, width)

    pieces = []
    for same in (True, False):
        mine, theirs = by_core(own, same), by_core(other, same)
        pieces += [jnp.where(first, mine, theirs), jnp.where(first, theirs, mine)]
    upstream = jnp.concatenate(pieces, axis=0)
    sigmoid_gate = jax.nn.sigmoid(gate_value)
    weighted = upstream * sigmoid_gate
    gate_grad = weighted * up_value * (1.0 + gate_value * (1.0 - sigmoid_gate))
    up_grad = weighted * gate_value
    grads_ref[:, :width] = gate_grad.astype(jnp.bfloat16)
    grads_ref[:, width:] = up_grad.astype(jnp.bfloat16)
    piece = rows // count

    def own_rows(values):
        near = jnp.where(first, values[:piece], values[piece : 2 * piece])
        away = jnp.where(first, values[2 * piece : 3 * piece], values[3 * piece :])
        near = near.reshape(piece // block_rows, 1, block_rows, width)
        away = away.reshape(piece // block_rows, 1, block_rows, width)
        both = jnp.concatenate(
            [jnp.where(even, near, away), jnp.where(even, away, near)], axis=1
        )
        return both.reshape(rows, width).astype(jnp.bfloat16)

    grads_own_ref[:, :width] = own_rows(gate_grad)
    grads_own_ref[:, width:] = own_rows(up_grad)
    block = blocks_of(factor, nz, far_ref.shape[0], normed_ref, grads_ref)
    far_ref[...] = block(nz // 2)
    for at, hub in enumerate(OUTER):
        outer_ahead_ref[at] = block(-hub - 1)
        outer_behind_ref[at] = block(-hub + 1)


def rest_kernel(
    factor,
    nz,
    normed_ref,
    grads_ref,
    grads_own_ref,
    gate_ref,
    up_ref,
    inner_ahead_ref,
    inner_behind_ref,
    outer_hub_ref,
    inner_hub_ref,
    part_ref,
):
    width = gate_ref.shape[0]
    block = blocks_of(factor, nz, outer_hub_ref.shape[1], normed_ref, grads_ref)
    for at, hub in enumerate(INNER):
        inner_ahead_ref[at] = block(-hub - 1)
        inner_behind_ref[at] = block(-hub + 1)
    for at, hub in enumerate(OUTER):
        outer_hub_ref[at] = block(hub)
    for at, hub in enumerate(INNER):
        inner_hub_ref[at] = block(hub)
    f32 = jnp.float32
    gate_part = jnp.dot(grads_own_ref[:, :width], gate_ref[...], preferred_element_type=f32)
    up_part = jnp.dot(grads_own_ref[:, width:], up_ref[...], preferred_element_type=f32)
    part_ref[...] = (gate_part + up_part).astype(jnp.bfloat16)


def f32_sum(*values):
    total = values[0].astype(jnp.float32)
    for value in values[1:]:
        total = total + value.astype(jnp.float32)
    return total


def outer_kernel(hub_ref, ahead_ref, behind_ref, far_ref, plus_ref, minus_ref):
    plus_ref[...] = f32_sum(hub_ref[0], ahead_ref[0], behind_ref[0]).astype(jnp.bfloat16)
    minus_ref[...] = f32_sum(hub_ref[1], ahead_ref[1], behind_ref[1], far_ref[...]).astype(
        jnp.bfloat16
    )


def inner_kernel(hub_ref, ahead_ref, behind_ref, upper_ref, lower_ref, plus_ref, minus_ref):
    plus_ref[...] = f32_sum(hub_ref[0], ahead_ref[0], behind_ref[0], lower_ref[...]).astype(
        jnp.bfloat16
    )
    minus_ref[...] = f32_sum(hub_ref[2], ahead_ref[2], behind_ref[2], upper_ref[...]).astype(
        jnp.bfloat16
    )


def total_kernel(hub_ref, ahead_ref, behind_ref, plus_ref, minus_ref, gate_ref, up_ref):
    width = gate_ref.shape[1]
    total = f32_sum(hub_ref[1], ahead_ref[1], behind_ref[1], plus_ref[...], minus_ref[...])
    gate_ref[...] = total[:, :width].astype(jnp.bfloat16)
    up_ref[...] = total[:, width:].astype(jnp.bfloat16)


def tail_kernel(rows_ref, gain_ref, moved_ref, out_ref):
    scaled, inverse = normalize(rows_ref[...])
    weighted = jnp.sum(moved_ref[...].astype(jnp.float32), axis=0) * gain_ref[...]
    mean = jnp.mean(weighted * scaled, axis=-1, keepdims=True)
    out_ref[...] = ((weighted - scaled * mean) * inverse).astype(jnp.bfloat16)


def call(kernel, name, shapes, *values):
    size = sum(value.size * 2 for value in values)
    return pl.pallas_call(
        kernel,
        out_shape=[jax.ShapeDtypeStruct(shape, jnp.bfloat16) for shape in shapes],
        compiler_params=pltpu.CompilerParams(vmem_limit_bytes=8 * 1024 * 1024),
        cost_estimate=pl.CostEstimate(flops=size, bytes_accessed=size, transcendentals=0),
        name=name,
    )(*values)


def norm_kernel(rows_ref, gain_ref, up_ref, normed_ref, value_ref):
    normed_ref[...] = (normalize(rows_ref[...])[0] * gain_ref[...]).astype(jnp.bfloat16)
    value_ref[...] = contract_last(normed_ref[...], up_ref[...])


def move(value, hops, nz):
    pairs = [(i, (i + (1 - 2 * (i % 2)) * hops) % nz) for i in range(nz)]
    return lax.ppermute(value, "z", pairs)


def shards(residual, norm_gain, gate_weight, up_weight, hidden_grad):
    nz, nh, nt = lax.axis_size("z"), lax.axis_size("yh"), lax.axis_size(TENSOR)
    rows, width = hidden_grad.shape
    features = residual.shape[1]
    depth = features // (nz * nh)
    f32, bf16 = jnp.float32, jnp.bfloat16
    own = hidden_grad
    other = lax.ppermute(own, "yh", [(0, 1), (1, 0)])
    chips = nh * nt // lax.axis_size("core")
    copies = jnp.broadcast_to(residual[None], (chips,) + residual.shape)
    same = lax.all_to_all(copies, ("yh", "x", "yl"), 0, 0, tiled=True)
    same = same.reshape(chips * residual.shape[0], features)
    same, other = lax.optimization_barrier((same, other))
    swapped = lax.ppermute(same, "core", [(0, 1), (1, 0)])
    gain = norm_gain.reshape(1, features)
    normed_same, up_same = pl.pallas_call(
        norm_kernel,
        out_shape=[
            jax.ShapeDtypeStruct(same.shape, bf16),
            jax.ShapeDtypeStruct((same.shape[0], width), f32),
        ],
        cost_estimate=pl.CostEstimate(
            flops=8 * rows * features, bytes_accessed=4 * rows * features, transcendentals=rows
        ),
        compiler_params=pltpu.CompilerParams(vmem_limit_bytes=8 * 1024 * 1024),
        name="norm",
    )(same, gain, up_weight.T)
    factor = float(rows * nz * nh) ** (-0.5)
    shape = jax.ShapeDtypeStruct
    wide = 2 * width
    far, outer_ahead, outer_behind, grads_own, normed, grads = pl.pallas_call(
        functools.partial(local_kernel, factor, nz, residual.shape[0]),
        out_shape=[
            jax.ShapeDtypeStruct(shape, bf16)
            for shape in (
                (depth, wide),
                (len(OUTER), depth, wide),
                (len(OUTER), depth, wide),
                (rows, wide),
                (nh * rows, features),
                (nh * rows, wide),
            )
        ],
        compiler_params=pltpu.CompilerParams(vmem_limit_bytes=20 * 1024 * 1024),
        cost_estimate=pl.CostEstimate(
            flops=6 * nh * rows * features * width,
            bytes_accessed=8 * features * width,
            transcendentals=nh * rows * width,
        ),
        name="local",
    )(normed_same, up_same, swapped, gain, gate_weight.T, up_weight.T, own, other)
    inner_ahead, inner_behind, outer_hub, inner_hub, part = pl.pallas_call(
        functools.partial(rest_kernel, factor, nz),
        out_shape=[
            jax.ShapeDtypeStruct((count, depth, wide), bf16)
            for count in (len(INNER), len(INNER), len(OUTER), len(INNER))
        ]
        + [jax.ShapeDtypeStruct((rows, features), bf16)],
        compiler_params=pltpu.CompilerParams(vmem_limit_bytes=16 * 1024 * 1024),
        cost_estimate=pl.CostEstimate(
            flops=6 * nh * rows * features * width,
            bytes_accessed=8 * nh * rows * features,
            transcendentals=0,
        ),
        name="rest",
    )(normed, grads, grads_own, gate_weight.T, up_weight.T)

    from_far = move(far, -2, nz).astype(f32)
    outer_ahead, outer_behind = move(outer_ahead, 1, nz), move(outer_behind, -1, nz)
    inner_ahead, inner_behind = move(inner_ahead, 1, nz), move(inner_behind, -1, nz)

    def outer(at):
        return (
            outer_hub[at].astype(f32)
            + outer_ahead[at].astype(f32)
            + outer_behind[at].astype(f32)
        )

    def inner(at, columns=slice(None)):
        return (
            inner_hub[at, :, columns].astype(f32)
            + inner_ahead[at, :, columns].astype(f32)
            + inner_behind[at, :, columns].astype(f32)
        )

    plus, minus = lax.optimization_barrier(
        (outer(0).astype(bf16), (outer(1) + from_far).astype(bf16))
    )
    part, first_sum = lax.optimization_barrier((part, plus))
    plus, minus = move(first_sum, 3, nz), move(minus, -3, nz)

    blocks = part.reshape(nt, rows // nt, features)
    moved = lax.all_to_all(blocks, TENSOR, 0, 0, tiled=True)

    plus, minus = lax.optimization_barrier((plus, minus))
    plus, minus = lax.optimization_barrier(
        (
            (inner(0) + minus.astype(f32)).astype(bf16),
            (inner(2) + plus.astype(f32)).astype(bf16),
        )
    )
    plus, minus = move(plus, 3, nz), move(minus, -3, nz)

    scaled, inverse = normalize(residual)
    normed_grad = jnp.sum(moved.astype(f32), axis=0)
    weighted = normed_grad * norm_gain
    residual_grad = (
        (weighted - scaled * jnp.mean(weighted * scaled, axis=-1, keepdims=True)) * inverse
    ).astype(bf16)
    totals = call(
        total_kernel,
        "total",
        [(depth, width)] * 2,
        inner_hub,
        inner_ahead,
        inner_behind,
        plus,
        minus,
    )
    return (residual_grad, totals[0], totals[1])


def solution(mesh):
    fine = Mesh(mesh.devices.reshape(16, 2, 4, 2, 2), DP + TENSOR)
    return jax.shard_map(
        shards,
        mesh=fine,
        in_specs=(
            P(DP + TENSOR, None),
            P(),
            P(None, TENSOR),
            P(None, TENSOR),
            P(DP, TENSOR),
        ),
        out_specs=(P(DP + TENSOR, None), P(DP, TENSOR), P(DP, TENSOR)),
        check_vma=False,
    )
```

```python
import functools

import jax
import jax.numpy as jnp
from jax import lax
from jax.experimental import pallas as pl
from jax.experimental.pallas import tpu as pltpu
from jax.sharding import Mesh
from jax.sharding import PartitionSpec as P

EPSILON = 1e-05
DP = ("z", "yh")
TENSOR = ("x", "yl", "core")
OUTER = (-6, 6)
INNER = (-3, 0, 3)


def normalize(residual):
    values = residual.astype(jnp.float32)
    inverse = lax.rsqrt(jnp.mean(values * values, axis=-1, keepdims=True) + EPSILON)
    return (values * inverse, inverse)


def contract_last(left, right):
    return lax.dot_general(
        left, right, (((1,), (1,)), ((), ())), preferred_element_type=jnp.float32
    )


def contract_first(left, right):
    return lax.dot_general(
        left, right, (((0,), (0,)), ((), ())), preferred_element_type=jnp.float32
    )


def blocks_of(factor, nz, depth, normed_ref, grads_ref):
    z = lax.axis_index("z")
    first = lax.axis_index("yh") == 0
    sign = 1 - 2 * lax.rem(z, 2)
    grads = grads_ref[...]

    def block(relative):
        chunk = lax.rem(z - sign * relative + 2 * nz, nz)
        lanes = pl.ds(pl.multiple_of(chunk * 2 * depth, 2 * depth), 2 * depth)
        both = contract_first(normed_ref[:, lanes], grads) * factor
        return jnp.where(first, both[:depth], both[depth:]).astype(jnp.bfloat16)

    return block


def local_kernel(
    factor,
    nz,
    block_rows,
    same_ref,
    up_same_ref,
    swapped_ref,
    gain_ref,
    gate_ref,
    up_ref,
    own_ref,
    other_ref,
    far_ref,
    outer_ahead_ref,
    outer_behind_ref,
    grads_own_ref,
    normed_ref,
    grads_ref,
):
    half = lax.axis_index("yh")
    rows, width = own_ref.shape
    tokens = same_ref.shape[0]
    normed_ref[:tokens] = same_ref[...]
    normed_ref[tokens:] = (normalize(swapped_ref[...])[0] * gain_ref[...]).astype(jnp.bfloat16)
    normed = normed_ref[...]
    gate_value = contract_last(normed, gate_ref[...])
    up_swapped = contract_last(normed_ref[tokens:], up_ref[...])
    up_value = jnp.concatenate([up_same_ref[...], up_swapped], axis=0)
    first = half == 0
    even = lax.axis_index("core") == 0
    count = lax.axis_size("core")
    split = (rows // (count * block_rows), count, block_rows, width)
    own = own_ref[...].astype(jnp.float32).reshape(split)
    other = other_ref[...].astype(jnp.float32).reshape(split)

    def by_core(values, same):
        near, away = (0, 1) if same else (1, 0)
        return jnp.where(even, values[:, near], values[:, away]).reshape(rows // count, width)

    pieces = []
    for same in (True, False):
        mine, theirs = by_core(own, same), by_core(other, same)
        pieces += [jnp.where(first, mine, theirs), jnp.where(first, theirs, mine)]
    upstream = jnp.concatenate(pieces, axis=0)
    sigmoid_gate = jax.nn.sigmoid(gate_value)
    weighted = upstream * sigmoid_gate
    gate_grad = weighted * up_value * (1.0 + gate_value * (1.0 - sigmoid_gate))
    up_grad = weighted * gate_value
    grads_ref[:, :width] = gate_grad.astype(jnp.bfloat16)
    grads_ref[:, width:] = up_grad.astype(jnp.bfloat16)
    piece = rows // count

    def own_rows(values):
        near = jnp.where(first, values[:piece], values[piece : 2 * piece])
        away = jnp.where(first, values[2 * piece : 3 * piece], values[3 * piece :])
        near = near.reshape(piece // block_rows, 1, block_rows, width)
        away = away.reshape(piece // block_rows, 1, block_rows, width)
        both = jnp.concatenate(
            [jnp.where(even, near, away), jnp.where(even, away, near)], axis=1
        )
        return both.reshape(rows, width).astype(jnp.bfloat16)

    grads_own_ref[:, :width] = own_rows(gate_grad)
    grads_own_ref[:, width:] = own_rows(up_grad)
    block = blocks_of(factor, nz, far_ref.shape[0], normed_ref, grads_ref)
    far_ref[...] = block(nz // 2)
    for at, hub in enumerate(OUTER):
        outer_ahead_ref[at] = block(-hub - 1)
        outer_behind_ref[at] = block(-hub + 1)


def rest_kernel(
    factor,
    nz,
    normed_ref,
    grads_ref,
    inner_ahead_ref,
    inner_behind_ref,
    outer_hub_ref,
    inner_hub_ref,
):
    block = blocks_of(factor, nz, outer_hub_ref.shape[1], normed_ref, grads_ref)
    for at, hub in enumerate(INNER):
        inner_ahead_ref[at] = block(-hub - 1)
        inner_behind_ref[at] = block(-hub + 1)
    for at, hub in enumerate(OUTER):
        outer_hub_ref[at] = block(hub)
    for at, hub in enumerate(INNER):
        inner_hub_ref[at] = block(hub)


def f32_sum(*values):
    total = values[0].astype(jnp.float32)
    for value in values[1:]:
        total = total + value.astype(jnp.float32)
    return total


def outer_kernel(hub_ref, ahead_ref, behind_ref, far_ref, plus_ref, minus_ref):
    plus_ref[...] = f32_sum(hub_ref[0], ahead_ref[0], behind_ref[0]).astype(jnp.bfloat16)
    minus_ref[...] = f32_sum(hub_ref[1], ahead_ref[1], behind_ref[1], far_ref[...]).astype(
        jnp.bfloat16
    )


def inner_kernel(hub_ref, ahead_ref, behind_ref, upper_ref, lower_ref, plus_ref, minus_ref):
    plus_ref[...] = f32_sum(hub_ref[0], ahead_ref[0], behind_ref[0], lower_ref[...]).astype(
        jnp.bfloat16
    )
    minus_ref[...] = f32_sum(hub_ref[2], ahead_ref[2], behind_ref[2], upper_ref[...]).astype(
        jnp.bfloat16
    )


def total_kernel(hub_ref, ahead_ref, behind_ref, plus_ref, minus_ref, gate_ref, up_ref):
    width = gate_ref.shape[1]
    total = f32_sum(hub_ref[1], ahead_ref[1], behind_ref[1], plus_ref[...], minus_ref[...])
    gate_ref[...] = total[:, :width].astype(jnp.bfloat16)
    up_ref[...] = total[:, width:].astype(jnp.bfloat16)


def tail_kernel(rows_ref, gain_ref, moved_ref, out_ref):
    scaled, inverse = normalize(rows_ref[...])
    weighted = jnp.sum(moved_ref[...].astype(jnp.float32), axis=0) * gain_ref[...]
    mean = jnp.mean(weighted * scaled, axis=-1, keepdims=True)
    out_ref[...] = ((weighted - scaled * mean) * inverse).astype(jnp.bfloat16)


def call(kernel, name, shapes, *values):
    size = sum(value.size * 2 for value in values)
    return pl.pallas_call(
        kernel,
        out_shape=[jax.ShapeDtypeStruct(shape, jnp.bfloat16) for shape in shapes],
        compiler_params=pltpu.CompilerParams(vmem_limit_bytes=8 * 1024 * 1024),
        cost_estimate=pl.CostEstimate(flops=size, bytes_accessed=size, transcendentals=0),
        name=name,
    )(*values)


def norm_kernel(rows_ref, gain_ref, up_ref, normed_ref, value_ref):
    normed_ref[...] = (normalize(rows_ref[...])[0] * gain_ref[...]).astype(jnp.bfloat16)
    value_ref[...] = contract_last(normed_ref[...], up_ref[...])


def move(value, hops, nz):
    pairs = [(i, (i + (1 - 2 * (i % 2)) * hops) % nz) for i in range(nz)]
    return lax.ppermute(value, "z", pairs)


def shards(residual, norm_gain, gate_weight, up_weight, hidden_grad):
    nz, nh, nt = lax.axis_size("z"), lax.axis_size("yh"), lax.axis_size(TENSOR)
    rows, width = hidden_grad.shape
    features = residual.shape[1]
    depth = features // (nz * nh)
    f32, bf16 = jnp.float32, jnp.bfloat16
    own = hidden_grad
    other = lax.ppermute(own, "yh", [(0, 1), (1, 0)])
    chips = nh * nt // lax.axis_size("core")
    copies = jnp.broadcast_to(residual[None], (chips,) + residual.shape)
    same = lax.all_to_all(copies, ("yh", "x", "yl"), 0, 0, tiled=True)
    same = same.reshape(chips * residual.shape[0], features)
    same, other = lax.optimization_barrier((same, other))
    swapped = lax.ppermute(same, "core", [(0, 1), (1, 0)])
    gain = norm_gain.reshape(1, features)
    normed_same, up_same = pl.pallas_call(
        norm_kernel,
        out_shape=[
            jax.ShapeDtypeStruct(same.shape, bf16),
            jax.ShapeDtypeStruct((same.shape[0], width), f32),
        ],
        cost_estimate=pl.CostEstimate(
            flops=8 * rows * features, bytes_accessed=4 * rows * features, transcendentals=rows
        ),
        compiler_params=pltpu.CompilerParams(vmem_limit_bytes=8 * 1024 * 1024),
        name="norm",
    )(same, gain, up_weight.T)
    factor = float(rows * nz * nh) ** (-0.5)
    shape = jax.ShapeDtypeStruct
    wide = 2 * width
    far, outer_ahead, outer_behind, grads_own, normed, grads = pl.pallas_call(
        functools.partial(local_kernel, factor, nz, residual.shape[0]),
        out_shape=[
            jax.ShapeDtypeStruct(shape, bf16)
            for shape in (
                (depth, wide),
                (len(OUTER), depth, wide),
                (len(OUTER), depth, wide),
                (rows, wide),
                (nh * rows, features),
                (nh * rows, wide),
            )
        ],
        compiler_params=pltpu.CompilerParams(vmem_limit_bytes=20 * 1024 * 1024),
        cost_estimate=pl.CostEstimate(
            flops=6 * nh * rows * features * width,
            bytes_accessed=8 * features * width,
            transcendentals=nh * rows * width,
        ),
        name="local",
    )(normed_same, up_same, swapped, gain, gate_weight.T, up_weight.T, own, other)
    inner_ahead, inner_behind, outer_hub, inner_hub = pl.pallas_call(
        functools.partial(rest_kernel, factor, nz),
        out_shape=[
            jax.ShapeDtypeStruct((count, depth, wide), bf16)
            for count in (len(INNER), len(INNER), len(OUTER), len(INNER))
        ],
        compiler_params=pltpu.CompilerParams(vmem_limit_bytes=12 * 1024 * 1024),
        cost_estimate=pl.CostEstimate(
            flops=4 * nh * rows * features * width,
            bytes_accessed=4 * nh * rows * features,
            transcendentals=0,
        ),
        name="rest",
    )(normed, grads)

    from_far = move(far, -2, nz).astype(f32)
    base = lax.optimization_barrier(outer_hub[1].astype(f32) + from_far)
    outer_ahead, outer_behind = move(outer_ahead, 1, nz), move(outer_behind, -1, nz)
    inner_ahead, inner_behind = move(inner_ahead, 1, nz), move(inner_behind, -1, nz)

    def outer(at):
        return (
            outer_hub[at].astype(f32)
            + outer_ahead[at].astype(f32)
            + outer_behind[at].astype(f32)
        )

    def inner(at, columns=slice(None)):
        return (
            inner_hub[at, :, columns].astype(f32)
            + inner_ahead[at, :, columns].astype(f32)
            + inner_behind[at, :, columns].astype(f32)
        )

    plus, minus = lax.optimization_barrier(
        (
            outer(0).astype(bf16),
            (base + outer_ahead[1].astype(f32) + outer_behind[1].astype(f32)).astype(bf16),
        )
    )
    grads_own, first_sum = lax.optimization_barrier((grads_own, plus))
    plus, minus = move(first_sum, 3, nz), move(minus, -3, nz)

    part = contract_last(grads_own[:, :width], gate_weight)
    part = (part + contract_last(grads_own[:, width:], up_weight)).astype(bf16)
    blocks = part.reshape(nt, rows // nt, features)
    moved = lax.all_to_all(blocks, TENSOR, 0, 0, tiled=True)

    plus, minus = lax.optimization_barrier((plus, minus))
    plus, minus = lax.optimization_barrier(
        (
            (inner(0) + minus.astype(f32)).astype(bf16),
            (inner(2) + plus.astype(f32)).astype(bf16),
        )
    )
    plus, minus = move(plus, 3, nz), move(minus, -3, nz)

    scaled, inverse = normalize(residual)
    normed_grad = jnp.sum(moved.astype(f32), axis=0)
    weighted = normed_grad * norm_gain
    residual_grad = (
        (weighted - scaled * jnp.mean(weighted * scaled, axis=-1, keepdims=True)) * inverse
    ).astype(bf16)
    totals = call(
        total_kernel,
        "total",
        [(depth, width)] * 2,
        inner_hub,
        inner_ahead,
        inner_behind,
        plus,
        minus,
    )
    return (residual_grad, totals[0], totals[1])


def solution(mesh):
    fine = Mesh(mesh.devices.reshape(16, 2, 4, 2, 2), DP + TENSOR)
    return jax.shard_map(
        shards,
        mesh=fine,
        in_specs=(
            P(DP + TENSOR, None),
            P(),
            P(None, TENSOR),
            P(None, TENSOR),
            P(DP, TENSOR),
        ),
        out_specs=(P(DP + TENSOR, None), P(DP, TENSOR), P(DP, TENSOR)),
        check_vma=False,
    )
```

```python
import functools

import jax
import jax.numpy as jnp
from jax import lax
from jax.experimental import pallas as pl
from jax.experimental.pallas import tpu as pltpu
from jax.sharding import Mesh
from jax.sharding import PartitionSpec as P

EPSILON = 1e-05
DP = ("z", "yh")
TENSOR = ("x", "yl", "core")
OUTER = (-6, 6)
INNER = (-3, 0, 3)


def normalize(residual):
    values = residual.astype(jnp.float32)
    inverse = lax.rsqrt(jnp.mean(values * values, axis=-1, keepdims=True) + EPSILON)
    return (values * inverse, inverse)


def contract_last(left, right):
    return lax.dot_general(
        left, right, (((1,), (1,)), ((), ())), preferred_element_type=jnp.float32
    )


def contract_first(left, right):
    return lax.dot_general(
        left, right, (((0,), (0,)), ((), ())), preferred_element_type=jnp.float32
    )


def blocks_of(factor, nz, depth, normed_ref, grads_ref):
    z = lax.axis_index("z")
    first = lax.axis_index("yh") == 0
    sign = 1 - 2 * lax.rem(z, 2)
    grads = grads_ref[...]

    def block(relative):
        chunk = lax.rem(z - sign * relative + 2 * nz, nz)
        lanes = pl.ds(pl.multiple_of(chunk * 2 * depth, 2 * depth), 2 * depth)
        both = contract_first(normed_ref[:, lanes], grads) * factor
        return jnp.where(first, both[:depth], both[depth:]).astype(jnp.bfloat16)

    return block


def local_kernel(
    factor,
    nz,
    block_rows,
    same_ref,
    up_same_ref,
    swapped_ref,
    gain_ref,
    gate_ref,
    up_ref,
    own_ref,
    other_ref,
    far_ref,
    outer_ahead_ref,
    outer_behind_ref,
    grads_own_ref,
    normed_ref,
    grads_ref,
):
    half = lax.axis_index("yh")
    rows, width = own_ref.shape
    tokens = same_ref.shape[0]
    normed_ref[:tokens] = same_ref[...]
    normed_ref[tokens:] = (normalize(swapped_ref[...])[0] * gain_ref[...]).astype(jnp.bfloat16)
    normed = normed_ref[...]
    gate_value = contract_last(normed, gate_ref[...])
    up_swapped = contract_last(normed_ref[tokens:], up_ref[...])
    up_value = jnp.concatenate([up_same_ref[...], up_swapped], axis=0)
    first = half == 0
    even = lax.axis_index("core") == 0
    count = lax.axis_size("core")
    split = (rows // (count * block_rows), count, block_rows, width)
    own = own_ref[...].astype(jnp.float32).reshape(split)
    other = other_ref[...].astype(jnp.float32).reshape(split)

    def by_core(values, same):
        near, away = (0, 1) if same else (1, 0)
        return jnp.where(even, values[:, near], values[:, away]).reshape(rows // count, width)

    pieces = []
    for same in (True, False):
        mine, theirs = by_core(own, same), by_core(other, same)
        pieces += [jnp.where(first, mine, theirs), jnp.where(first, theirs, mine)]
    upstream = jnp.concatenate(pieces, axis=0)
    sigmoid_gate = jax.nn.sigmoid(gate_value)
    weighted = upstream * sigmoid_gate
    gate_grad = weighted * up_value * (1.0 + gate_value * (1.0 - sigmoid_gate))
    up_grad = weighted * gate_value
    grads_ref[:, :width] = gate_grad.astype(jnp.bfloat16)
    grads_ref[:, width:] = up_grad.astype(jnp.bfloat16)
    piece = rows // count

    def own_rows(values):
        near = jnp.where(first, values[:piece], values[piece : 2 * piece])
        away = jnp.where(first, values[2 * piece : 3 * piece], values[3 * piece :])
        near = near.reshape(piece // block_rows, 1, block_rows, width)
        away = away.reshape(piece // block_rows, 1, block_rows, width)
        both = jnp.concatenate(
            [jnp.where(even, near, away), jnp.where(even, away, near)], axis=1
        )
        return both.reshape(rows, width).astype(jnp.bfloat16)

    grads_own_ref[:, :width] = own_rows(gate_grad)
    grads_own_ref[:, width:] = own_rows(up_grad)
    block = blocks_of(factor, nz, far_ref.shape[0], normed_ref, grads_ref)
    far_ref[...] = block(nz // 2)
    for at, hub in enumerate(OUTER):
        outer_ahead_ref[at] = block(-hub - 1)
        outer_behind_ref[at] = block(-hub + 1)


def rest_kernel(
    factor,
    nz,
    normed_ref,
    grads_ref,
    grads_own_ref,
    gate_ref,
    up_ref,
    inner_ahead_ref,
    inner_behind_ref,
    outer_hub_ref,
    inner_hub_ref,
    part_ref,
):
    width = gate_ref.shape[0]
    block = blocks_of(factor, nz, outer_hub_ref.shape[1], normed_ref, grads_ref)
    for at, hub in enumerate(INNER):
        inner_ahead_ref[at] = block(-hub - 1)
        inner_behind_ref[at] = block(-hub + 1)
    for at, hub in enumerate(OUTER):
        outer_hub_ref[at] = block(hub)
    for at, hub in enumerate(INNER):
        inner_hub_ref[at] = block(hub)
    f32 = jnp.float32
    gate_part = jnp.dot(grads_own_ref[:, :width], gate_ref[...], preferred_element_type=f32)
    up_part = jnp.dot(grads_own_ref[:, width:], up_ref[...], preferred_element_type=f32)
    part_ref[...] = (gate_part + up_part).astype(jnp.bfloat16)


def f32_sum(*values):
    total = values[0].astype(jnp.float32)
    for value in values[1:]:
        total = total + value.astype(jnp.float32)
    return total


def outer_kernel(hub_ref, ahead_ref, behind_ref, far_ref, plus_ref, minus_ref):
    plus_ref[...] = f32_sum(hub_ref[0], ahead_ref[0], behind_ref[0]).astype(jnp.bfloat16)
    minus_ref[...] = f32_sum(hub_ref[1], ahead_ref[1], behind_ref[1], far_ref[...]).astype(
        jnp.bfloat16
    )


def inner_kernel(hub_ref, ahead_ref, behind_ref, upper_ref, lower_ref, plus_ref, minus_ref):
    plus_ref[...] = f32_sum(hub_ref[0], ahead_ref[0], behind_ref[0], lower_ref[...]).astype(
        jnp.bfloat16
    )
    minus_ref[...] = f32_sum(hub_ref[2], ahead_ref[2], behind_ref[2], upper_ref[...]).astype(
        jnp.bfloat16
    )


def total_kernel(hub_ref, ahead_ref, behind_ref, plus_ref, minus_ref, gate_ref, up_ref):
    width = gate_ref.shape[1]
    total = f32_sum(hub_ref[1], ahead_ref[1], behind_ref[1], plus_ref[...], minus_ref[...])
    gate_ref[...] = total[:, :width].astype(jnp.bfloat16)
    up_ref[...] = total[:, width:].astype(jnp.bfloat16)


def tail_kernel(rows_ref, gain_ref, moved_ref, out_ref):
    scaled, inverse = normalize(rows_ref[...])
    weighted = jnp.sum(moved_ref[...].astype(jnp.float32), axis=0) * gain_ref[...]
    mean = jnp.mean(weighted * scaled, axis=-1, keepdims=True)
    out_ref[...] = ((weighted - scaled * mean) * inverse).astype(jnp.bfloat16)


def call(kernel, name, shapes, *values):
    size = sum(value.size * 2 for value in values)
    return pl.pallas_call(
        kernel,
        out_shape=[jax.ShapeDtypeStruct(shape, jnp.bfloat16) for shape in shapes],
        compiler_params=pltpu.CompilerParams(vmem_limit_bytes=8 * 1024 * 1024),
        cost_estimate=pl.CostEstimate(flops=size, bytes_accessed=size, transcendentals=0),
        name=name,
    )(*values)


def norm_kernel(rows_ref, gain_ref, up_ref, normed_ref, value_ref):
    normed_ref[...] = (normalize(rows_ref[...])[0] * gain_ref[...]).astype(jnp.bfloat16)
    value_ref[...] = contract_last(normed_ref[...], up_ref[...])


def move(value, hops, nz):
    pairs = [(i, (i + (1 - 2 * (i % 2)) * hops) % nz) for i in range(nz)]
    return lax.ppermute(value, "z", pairs)


def shards(residual, norm_gain, gate_weight, up_weight, hidden_grad):
    nz, nh, nt = lax.axis_size("z"), lax.axis_size("yh"), lax.axis_size(TENSOR)
    rows, width = hidden_grad.shape
    features = residual.shape[1]
    depth = features // (nz * nh)
    f32, bf16 = jnp.float32, jnp.bfloat16
    own = hidden_grad
    other = lax.ppermute(own, "yh", [(0, 1), (1, 0)])
    chips = nh * nt // lax.axis_size("core")
    copies = jnp.broadcast_to(residual[None], (chips,) + residual.shape)
    same = lax.all_to_all(copies, ("yh", "x", "yl"), 0, 0, tiled=True)
    same = same.reshape(chips * residual.shape[0], features)
    same, other = lax.optimization_barrier((same, other))
    swapped = lax.ppermute(same, "core", [(0, 1), (1, 0)])
    gain = norm_gain.reshape(1, features)
    normed_same, up_same = pl.pallas_call(
        norm_kernel,
        out_shape=[
            jax.ShapeDtypeStruct(same.shape, bf16),
            jax.ShapeDtypeStruct((same.shape[0], width), f32),
        ],
        cost_estimate=pl.CostEstimate(
            flops=8 * rows * features, bytes_accessed=4 * rows * features, transcendentals=rows
        ),
        compiler_params=pltpu.CompilerParams(vmem_limit_bytes=8 * 1024 * 1024),
        name="norm",
    )(same, gain, up_weight.T)
    factor = float(rows * nz * nh) ** (-0.5)
    shape = jax.ShapeDtypeStruct
    wide = 2 * width
    far, outer_ahead, outer_behind, grads_own, normed, grads = pl.pallas_call(
        functools.partial(local_kernel, factor, nz, residual.shape[0]),
        out_shape=[
            jax.ShapeDtypeStruct(shape, bf16)
            for shape in (
                (depth, wide),
                (len(OUTER), depth, wide),
                (len(OUTER), depth, wide),
                (rows, wide),
                (nh * rows, features),
                (nh * rows, wide),
            )
        ],
        compiler_params=pltpu.CompilerParams(vmem_limit_bytes=20 * 1024 * 1024),
        cost_estimate=pl.CostEstimate(
            flops=6 * nh * rows * features * width,
            bytes_accessed=8 * features * width,
            transcendentals=nh * rows * width,
        ),
        name="local",
    )(normed_same, up_same, swapped, gain, gate_weight.T, up_weight.T, own, other)
    inner_ahead, inner_behind, outer_hub, inner_hub, part = pl.pallas_call(
        functools.partial(rest_kernel, factor, nz),
        out_shape=[
            jax.ShapeDtypeStruct((count, depth, wide), bf16)
            for count in (len(INNER), len(INNER), len(OUTER), len(INNER))
        ]
        + [jax.ShapeDtypeStruct((rows, features), bf16)],
        compiler_params=pltpu.CompilerParams(vmem_limit_bytes=16 * 1024 * 1024),
        cost_estimate=pl.CostEstimate(
            flops=6 * nh * rows * features * width,
            bytes_accessed=8 * nh * rows * features,
            transcendentals=0,
        ),
        name="rest",
    )(normed, grads, grads_own, gate_weight.T, up_weight.T)

    from_far = move(far, -2, nz).astype(f32)
    base = lax.optimization_barrier(outer_hub[1].astype(f32) + from_far)
    outer_ahead, outer_behind = move(outer_ahead, 1, nz), move(outer_behind, -1, nz)
    inner_ahead, inner_behind = move(inner_ahead, 1, nz), move(inner_behind, -1, nz)

    def outer(at):
        return (
            outer_hub[at].astype(f32)
            + outer_ahead[at].astype(f32)
            + outer_behind[at].astype(f32)
        )

    def inner(at, columns=slice(None)):
        return (
            inner_hub[at, :, columns].astype(f32)
            + inner_ahead[at, :, columns].astype(f32)
            + inner_behind[at, :, columns].astype(f32)
        )

    plus, minus = lax.optimization_barrier(
        (
            outer(0).astype(bf16),
            (base + outer_ahead[1].astype(f32) + outer_behind[1].astype(f32)).astype(bf16),
        )
    )
    part, first_sum = lax.optimization_barrier((part, plus))
    plus, minus = move(first_sum, 3, nz), move(minus, -3, nz)

    blocks = part.reshape(nt, rows // nt, features)
    moved = lax.all_to_all(blocks, TENSOR, 0, 0, tiled=True)

    plus, minus = lax.optimization_barrier((plus, minus))
    plus, minus = lax.optimization_barrier(
        (
            (inner(0) + minus.astype(f32)).astype(bf16),
            (inner(2) + plus.astype(f32)).astype(bf16),
        )
    )
    plus, minus = move(plus, 3, nz), move(minus, -3, nz)

    scaled, inverse = normalize(residual)
    normed_grad = jnp.sum(moved.astype(f32), axis=0)
    weighted = normed_grad * norm_gain
    residual_grad = (
        (weighted - scaled * jnp.mean(weighted * scaled, axis=-1, keepdims=True)) * inverse
    ).astype(bf16)
    totals = call(
        total_kernel,
        "total",
        [(depth, width)] * 2,
        inner_hub,
        inner_ahead,
        inner_behind,
        plus,
        minus,
    )
    return (residual_grad, totals[0], totals[1])


def solution(mesh):
    fine = Mesh(mesh.devices.reshape(16, 2, 4, 2, 2), DP + TENSOR)
    return jax.shard_map(
        shards,
        mesh=fine,
        in_specs=(
            P(DP + TENSOR, None),
            P(),
            P(None, TENSOR),
            P(None, TENSOR),
            P(DP, TENSOR),
        ),
        out_specs=(P(DP + TENSOR, None), P(DP, TENSOR), P(DP, TENSOR)),
        check_vma=False,
    )
```
